256 devices in a mesh: blk: 64 (over x_lo, y, z), sec: 4 (over x_hi, core).
Axes of the slice: x: 4 (x_hi: 2, x_lo: 2; x = x_hi * 2 + x_lo), y: 4, z: 8, core: 2. Of those that a mesh axis runs over, the one named last changes fastest.
Arguments:
- factors: bfloat16 [64, 512, 1024], P('blk', None, 'sec'), may hold values from -0.5 to 0.5
- occ_energy: float32 [64], replicated, may hold values from -2 to -0.5
- vir_energy: float32 [512], replicated, may hold values from 0.2 to 3
- metric: float32 [1024, 1024], replicated, may hold values from -0.1875 to 0.1875
Outputs:
- gamma: float32 [1024, 64, 512], P('sec', 'blk')
- density: float32 [512, 512], P('blk')
The draws below stay inside these ranges and needn't reach their ends.
All inputs are finite; a program needn't handle non-finite values.
Results may differ from the reference program's by a relative error of at most 0.00077.
Values may be sent and summed in bfloat16 or wider, within the bound.
A program may use at most 64 MiB of HBM per device.

```python
import jax
import jax.numpy as jnp
from jax import lax

V = 512
NAUX = 1024
OCC = 1
NO = 64
STEPS = 4
N_BLK = 64
N_SEC = 4


def block_levels(stream_key, extent, cuts, least, top_value):
    def one(axis_at, blocks):
        heights = jax.random.uniform(jax.random.fold_in(jax.random.fold_in(stream_key, 6), axis_at), (blocks,), jnp.float32, least / len(cuts), top_value / len(cuts))
        return jnp.repeat(jnp.exp(heights), extent[axis_at] // blocks).reshape((-1,) + (1,) * (len(extent) - axis_at - 1))

    factor_of = one(*cuts[0])
    for cut in cuts[1:]:
        factor_of = factor_of * one(*cut)
    return factor_of


def noise(own_key, shape, scale, reach, shards=(), dtype=jnp.bfloat16):
    values = scale * jax.random.normal(own_key, shape, jnp.float32)
    if shards:
        values = values * block_levels(own_key, shape, shards, -0.22, 0.18)
    return jnp.clip(values, -reach, reach).astype(dtype)


def setup_inputs(seed: int = 0) -> dict:
    arg_keys = jax.random.split(jax.random.key(seed), 5)
    factors = noise(arg_keys[0], (NO, V, NAUX), (V // 4) ** -0.5, 0.5, ((0, 64), (2, 4)))
    occ_energy = jnp.clip(jax.random.uniform(arg_keys[1], (NO,), jnp.float32, -2.0, -0.5), -2.0, -0.5)
    vir_energy = jnp.clip(jax.random.uniform(arg_keys[2], (V,), jnp.float32, 0.2, 3.0), 0.2, 3.0)
    metric = noise(arg_keys[3], (NAUX, NAUX), NAUX ** -0.5, 0.1875, (), jnp.float32)
    return dict(factors=factors, occ_energy=occ_energy, vir_energy=vir_energy, metric=metric)


def reference(factors, occ_energy, vir_energy, metric):
    window = STEPS * N_SEC
    orbitals = factors.shape[0]
    accumulated = jnp.zeros((orbitals, V, NAUX), jnp.float32)
    density = jnp.zeros((V, V), jnp.float32)
    total = N_BLK * window * OCC * OCC

    def one_pair(pair_index, loop_state):
        accumulated, density = loop_state
        first_pos = pair_index % OCC
        rest = pair_index // OCC
        second = rest % OCC
        rest = rest // OCC
        offset = rest % window
        batch_index = rest // window
        first_orb = (batch_index * OCC + first_pos).astype(jnp.int32)
        second_orb = (((batch_index - offset) % N_BLK) * OCC + second).astype(jnp.int32)
        left_block = lax.dynamic_index_in_dim(factors, first_orb, 0, keepdims=False).astype(jnp.float32)
        right_block = lax.dynamic_index_in_dim(factors, second_orb, 0, keepdims=False).astype(jnp.float32)
        intersection = jnp.dot(left_block, right_block.T, precision=lax.Precision.HIGHEST, preferred_element_type=jnp.float32)
        energy_sum = lax.dynamic_index_in_dim(occ_energy, first_orb, 0, keepdims=False) + lax.dynamic_index_in_dim(occ_energy, second_orb, 0, keepdims=False)
        denominator = energy_sum - vir_energy[:, None] - vir_energy[None, :]
        amplitude = intersection / denominator
        mixed_amp = 2.0 * amplitude - amplitude.T
        amp_half = lax.optimization_barrier(amplitude.astype(jnp.bfloat16)).astype(jnp.float32)
        mixed_half = lax.optimization_barrier(mixed_amp.astype(jnp.bfloat16)).astype(jnp.float32)
        weight = jnp.where(offset == 0, jnp.float32(0.5), jnp.float32(1.0))
        own_term = jnp.dot(mixed_half, right_block, precision=lax.Precision.HIGHEST, preferred_element_type=jnp.float32)
        part_term = jnp.dot(mixed_half.T, left_block, precision=lax.Precision.HIGHEST, preferred_element_type=jnp.float32)
        accumulated = accumulated.at[first_orb].add(weight * own_term)
        accumulated = accumulated.at[second_orb].add(weight * part_term)
        dens_term = jnp.dot(mixed_half, amp_half.T, precision=lax.Precision.HIGHEST, preferred_element_type=jnp.float32)
        dens_term = dens_term + jnp.dot(mixed_half.T, amp_half, precision=lax.Precision.HIGHEST, preferred_element_type=jnp.float32)
        density = density + weight * dens_term
        return accumulated, density

    accumulated, density = lax.fori_loop(0, total, one_pair, (accumulated, density))
    gamma = jnp.einsum("pq,iap->qia", metric.astype(jnp.float32), accumulated, precision=lax.Precision.HIGHEST)
    return gamma, density
```

```python
import jax
import jax.numpy as jnp
from jax import lax
from jax.experimental import pallas as pl
from jax.experimental.pallas import tpu as pltpu
from jax.sharding import PartitionSpec as P

MESH = pl.DeviceIdType.MESH
F32 = jnp.float32
BF16 = jnp.bfloat16
NT = (((1,), (1,)), ((), ()))
NN = (((1,), (0,)), ((), ()))

V = 512
QW = 256
NB = 64
STEPS = 8
ROWS = 256


def dot(a, b, dims):
    return lax.dot_general(a, b, dims, preferred_element_type=F32)


def kernel(
    occ_ref,
    f_ref,
    vir_ref,
    metric_ref,
    gamma_ref,
    dens_out_ref,
    slots,
    g_acc,
    dens,
    vir_sum,
    t_buf,
    tb_buf,
    m_f32,
    m_hi,
    m_lo,
    g_hi,
    g_lo,
    part,
    ra,
    rb,
    rx,
    dr0,
    d1,
    dry,
    d2,
    drz,
    d3,
    drx,
    d4,
    dr4,
    local_sem,
    init_ssem,
    ssem,
    rsem,
    tail_ssem,
    tail_rsem,
    y_ssem,
    y_rsem,
    z_ssem,
    z_rsem,
    x_ssem,
    x_rsem,
):
    b = lax.axis_index("blk")
    s = lax.axis_index("sec")
    x_hi = s // 2
    core = s % 2
    x_lo = b // 32
    y = (b // 8) % 4
    z = b % 8
    far = s // 2
    mate = s + 1 - 2 * core
    across = (s + 2) % 4
    diag = 3 - s
    sign = 1 - 2 * core
    nxt = (b + sign + NB) % NB
    prv = (b - sign + NB) % NB

    def y_peer(i):
        yy = (y + i) % 4
        return yy, (x_lo * 32 + yy * 8 + z, s)

    def z_peer(i):
        zz = (z + i) % 8
        return zz, (x_lo * 32 + y * 8 + zz, s)

    def x_peer(i):
        xx = (x_hi * 2 + x_lo + i) % 4
        return xx, ((xx % 2) * 32 + y * 8 + z, (xx // 2) * 2 + core)

    barrier = pltpu.get_barrier_semaphore()

    def greet(dev):
        pl.semaphore_signal(barrier, inc=1, device_id=dev, device_id_type=MESH)

    for t in (mate, across, diag):
        greet((b, t))
    greet((nxt, s))
    greet((prv, s))
    greet(((b + 8) % NB, 2))
    greet(((b + NB - 8) % NB, 3))

    @pl.when(far == 1)
    def _():
        source = (b - 8 * sign + NB) % NB
        for t in range(4):
            greet((source, t))

    for i in (1, 2, 3):
        greet(y_peer(i)[1])
    for i in range(1, 8):
        greet(z_peer(i)[1])
    for i in (1, 3):
        greet(x_peer(i)[1])

    metric_copy = pltpu.make_async_copy(metric_ref, m_f32, local_sem.at[1])
    metric_copy.start()
    own_copy = pltpu.make_async_copy(f_ref.at[0], slots.at[0, s], local_sem.at[0])
    own_copy.start()

    pl.semaphore_wait(barrier, 19 + 4 * far)

    def remote(src, dst, send, recv, dev):
        return pltpu.make_async_remote_copy(
            src_ref=src, dst_ref=dst, send_sem=send, recv_sem=recv,
            device_id=dev, device_id_type=MESH,
        )

    firsts = []
    for i, (dev, entry) in enumerate(
        (
            ((b, across), 0),
            ((b, mate), 0),
            ((b, diag), 0),
            (((b + 8) % NB, 2), 8),
            (((b + NB - 8) % NB, 3), 8),
        )
    ):
        c = remote(f_ref.at[0], slots.at[entry, s], init_ssem.at[i], rsem.at[entry, s], dev)
        c.start()
        firsts.append(c)

    def hop(src_entry, dst_entry, q):
        return remote(
            slots.at[src_entry, q], slots.at[dst_entry, q],
            ssem.at[dst_entry, q], rsem.at[dst_entry, q], (nxt, s),
        )

    def arrived(entry, q):
        remote(
            slots.at[entry, q], slots.at[entry, q],
            ssem.at[entry, q], rsem.at[entry, q], (nxt, s),
        ).wait_recv()

    order = (s, mate, across, diag)

    own_copy.wait()

    @pl.when(far == 0)
    def _():
        for n, q in enumerate(order):
            if n > 0:
                arrived(0, q)
            hop(0, 1, q).start()

    @pl.when(far == 1)
    def _():
        for q in order:
            arrived(8, q)
            hop(8, 1, q).start()
        for q in order[1:]:
            arrived(0, q)

    vir_rows = jnp.broadcast_to(vir_ref[...], (V, V))
    vir_sum[...] = vir_rows + vir_rows.T
    g_acc[...] = jnp.zeros_like(g_acc)
    dens[...] = jnp.zeros_like(dens)
    metric_copy.wait()
    for i in range(4):
        rows = pl.ds(i * QW, QW)
        m = m_f32[rows, :]
        hi = m.astype(BF16)
        m_hi[rows, :] = hi
        m_lo[rows, :] = (m - hi.astype(F32)).astype(BF16)

    own_e = occ_ref[b]

    def pair(entry, offset):
        e_sum = own_e + occ_ref[(b - sign * offset + 2 * NB) % NB]
        for rc in range(V // ROWS):
            rows = pl.ds(rc * ROWS, ROWS)
            acc = dot(slots[0, 0, rows, :], slots[entry, 0], NT)
            for q in range(1, 4):
                acc = acc + dot(slots[0, q, rows, :], slots[entry, q], NT)
            t = acc / (e_sum - vir_sum[rows, :])
            t_buf[rows, :] = t
            tb_buf[rows, :] = t.astype(BF16)
        for rc in range(V // ROWS):
            rows = pl.ds(rc * ROWS, ROWS)
            ub = (2.0 * t_buf[rows, :] - t_buf[:, rows].T).astype(BF16)
            for q in range(4):
                g_acc[q, rows, :] += dot(ub, slots[entry, q], NN)
            for h in range(2):
                dens[h, rows, :] += dot(ub, tb_buf[pl.ds(h * QW, QW), :], NT)

    @pl.when(s != 1)
    def _():
        pair(8 * far, 8 * far)

    def step(k, carry):
        for q in order:
            arrived(k, q)

            @pl.when(k < STEPS - 1)
            def _():
                hop(k, k + 1, q).start()

        pair(k, k + 8 * far)
        return carry

    lax.fori_loop(1, STEPS, step, 0)

    sends = []

    def send(src, dst, ss, rs, dev):
        c = remote(src, dst, ss, rs, dev)
        c.start()
        sends.append(c)
        return c

    c_d0 = send(dens.at[1 - core], dr0, tail_ssem.at[0], tail_rsem.at[0], (b, mate))

    for q in range(4):
        g = g_acc[q]
        hi = g.astype(BF16)
        g_hi[q] = hi
        g_lo[q] = (g - hi.astype(F32)).astype(BF16)

    def metric_part(t):
        cols = pl.ds(pl.multiple_of(t * QW, QW), QW)
        acc = None
        for q in range(4):
            rows = pl.ds(q * QW, QW)
            mh = m_hi[rows, cols]
            ml = m_lo[rows, cols]
            term = dot(g_hi[q], mh, NN) + (dot(g_lo[q], mh, NN) + dot(g_hi[q], ml, NN))
            acc = term if acc is None else acc + term
        return acc

    part[0] = metric_part(diag)
    c_a = send(part.at[0], ra, tail_ssem.at[1], tail_rsem.at[1], (b, mate))

    c_d0.wait_recv()
    for xl in range(2):
        for yy in range(4):
            rows = pl.ds(xl * 256 + yy * 64, 64)
            d1[yy, xl] = dens[core, rows, :] + dr0[rows, :]
    y_copies = []
    for i in (1, 2, 3):
        yy, dev = y_peer(i)
        y_copies.append(send(d1.at[yy], dry.at[y], y_ssem.at[i], y_rsem.at[y], dev))

    p_across = metric_part(across)
    c_a.wait_recv()
    part[1] = p_across + ra[...]
    c_x = send(part.at[1], rx, tail_ssem.at[2], tail_rsem.at[2], (b, across))

    part[2] = metric_part(mate)
    c_b = send(part.at[2], rb, tail_ssem.at[3], tail_rsem.at[3], (b, mate))

    total = d1[y]
    for i in (1, 2, 3):
        yy, dev = y_peer(i)
        remote(d1.at[yy], dry.at[yy], y_ssem.at[i], y_rsem.at[yy], dev).wait_recv()
        total = total + dry[yy]
    for zz in range(8):
        d2[zz] = total[:, zz * 8 : zz * 8 + 8, :]
    for i in range(1, 8):
        zz, dev = z_peer(i)
        send(d2.at[zz], drz.at[z], z_ssem.at[i], z_rsem.at[z], dev)

    mine = metric_part(s)

    total = d2[z]
    for i in range(1, 8):
        zz, dev = z_peer(i)
        remote(d2.at[zz], drz.at[zz], z_ssem.at[i], z_rsem.at[zz], dev).wait_recv()
        total = total + drz[zz]
    d3[...] = total
    here = x_hi * 2 + x_lo
    for i in (1, 2, 3):
        xx, dev = x_peer(i)
        send(d3.at[xx % 2], drx.at[here], x_ssem.at[i], x_rsem.at[here], dev)
    drx[here] = d3[x_lo]

    c_b.wait_recv()
    part[3] = mine + rb[...]

    for i in (1, 2, 3):
        xx, dev = x_peer(i)
        remote(d3.at[0], drx.at[xx], x_ssem.at[i], x_rsem.at[xx], dev).wait_recv()
    d4[...] = (drx[0] + drx[1]) + (drx[2] + drx[3])
    c_4 = send(d4, dr4, tail_ssem.at[4], tail_rsem.at[4], (b, mate))
    c_4.wait_recv()

    @pl.when(core == 0)
    def _():
        dens_out_ref[:, pl.ds(0, QW)] = d4[...]
        dens_out_ref[:, pl.ds(QW, QW)] = dr4[...]

    @pl.when(core == 1)
    def _():
        dens_out_ref[:, pl.ds(0, QW)] = dr4[...]
        dens_out_ref[:, pl.ds(QW, QW)] = d4[...]

    c_x.wait_recv()
    gamma_ref[...] = (part[3] + rx[...]).T

    for c in firsts:
        c.wait_send()

    def drain(k, carry):
        for q in range(4):
            hop(k - 1, k, q).wait_send()
        return carry

    lax.fori_loop(1, STEPS, drain, 0)
    for c in sends:
        c.wait_send()


def per_device(factors, occ_energy, vir_energy, metric):
    vmem = pl.BlockSpec(memory_space=pltpu.VMEM)
    dma = pltpu.SemaphoreType.DMA
    gamma, density = pl.pallas_call(
        kernel,
        out_shape=(
            jax.ShapeDtypeStruct((QW, V), F32),
            jax.ShapeDtypeStruct((8, V), F32),
        ),
        in_specs=[
            pl.BlockSpec(memory_space=pltpu.SMEM),
            vmem,
            vmem,
            pl.BlockSpec(memory_space=pl.ANY),
        ],
        out_specs=(vmem, vmem),
        scratch_shapes=[
            pltpu.VMEM((9, 4, V, QW), BF16),
            pltpu.VMEM((4, V, QW), F32),
            pltpu.VMEM((2, V, QW), F32),
            pltpu.VMEM((V, V), F32),
            pltpu.VMEM((V, V), F32),
            pltpu.VMEM((V, V), BF16),
            pltpu.VMEM((4 * QW, 4 * QW), F32),
            pltpu.VMEM((4 * QW, 4 * QW), BF16),
            pltpu.VMEM((4 * QW, 4 * QW), BF16),
            pltpu.VMEM((4, V, QW), BF16),
            pltpu.VMEM((4, V, QW), BF16),
            pltpu.VMEM((4, V, QW), F32),
            pltpu.VMEM((V, QW), F32),
            pltpu.VMEM((V, QW), F32),
            pltpu.VMEM((V, QW), F32),
            pltpu.VMEM((V, QW), F32),
            pltpu.VMEM((4, 2, 64, QW), F32),
            pltpu.VMEM((4, 2, 64, QW), F32),
            pltpu.VMEM((8, 2, 8, QW), F32),
            pltpu.VMEM((8, 2, 8, QW), F32),
            pltpu.VMEM((2, 8, QW), F32),
            pltpu.VMEM((4, 8, QW), F32),
            pltpu.VMEM((8, QW), F32),
            pltpu.VMEM((8, QW), F32),
            dma((2,)),
            dma((5,)),
            dma((9, 4)),
            dma((9, 4)),
            dma((5,)),
            dma((5,)),
            dma((4,)),
            dma((4,)),
            dma((8,)),
            dma((8,)),
            dma((4,)),
            dma((4,)),
        ],
        compiler_params=pltpu.CompilerParams(
            collective_id=0, has_side_effects=True, vmem_limit_bytes=60 * 1024 * 1024
        ),
    )(occ_energy, factors, vir_energy.reshape(1, V), metric)
    return gamma.reshape(QW, 1, V), density


def solution(mesh):
    return jax.shard_map(
        per_device,
        mesh=mesh,
        in_specs=(P("blk", None, "sec"), P(), P(), P()),
        out_specs=(P("sec", "blk", None), P("blk", None)),
        check_vma=False,
    )
```

```python
import jax
import jax.numpy as jnp
from jax import lax
from jax.experimental import pallas as pl
from jax.experimental.pallas import tpu as pltpu
from jax.sharding import PartitionSpec as P

MESH = pl.DeviceIdType.MESH
F32 = jnp.float32
BF16 = jnp.bfloat16
NT = (((1,), (1,)), ((), ()))
NN = (((1,), (0,)), ((), ()))

V = 512
QW = 256
NB = 64
ROWS = 256


def dot(a, b, dims):
    return lax.dot_general(a, b, dims, preferred_element_type=F32)


def kernel(
    occ_ref,
    f_ref,
    vir_ref,
    metric_ref,
    gamma_ref,
    dens_out_ref,
    jb,
    rbuf,
    g_acc,
    dens,
    vir_sum,
    t_buf,
    tb_buf,
    m_f32,
    m_hi,
    m_lo,
    g_hi,
    g_lo,
    part,
    ra,
    rb,
    rx,
    dr0,
    d1,
    dry,
    d2,
    drz,
    d3,
    drx,
    d4,
    dr4,
    local_sem,
    init_ssem,
    zinit_ssem,
    z_fwd,
    zr_fwd,
    y_fwd,
    rsem,
    rrsem,
    tail_ssem,
    tail_rsem,
    y_ssem,
    y_rsem,
    z_ssem,
    z_rsem,
    x_ssem,
    x_rsem,
):
    b = lax.axis_index("blk")
    s = lax.axis_index("sec")
    x_hi = s // 2
    core = s % 2
    x_lo = b // 32
    y = (b // 8) % 4
    z = b % 8
    mate = s + 1 - 2 * core
    across = (s + 2) % 4
    diag = 3 - s

    def y_peer(i):
        yy = (y + i) % 4
        return yy, (x_lo * 32 + yy * 8 + z, s)

    def z_peer(i):
        zz = (z + i + 8) % 8
        return zz, (x_lo * 32 + y * 8 + zz, s)

    def x_peer(i):
        xx = (x_hi * 2 + x_lo + i) % 4
        return xx, ((xx % 2) * 32 + y * 8 + z, (xx // 2) * 2 + core)

    def row_peer(rows, sec):
        return ((b + 8 * rows + NB) % NB, sec)

    barrier = pltpu.get_barrier_semaphore()

    def greet(dev):
        pl.semaphore_signal(barrier, inc=1, device_id=dev, device_id_type=MESH)

    greet((b, mate))
    for i in (1, 2, 3):
        greet(x_peer(i)[1])
    for c in range(2):
        greet(row_peer(1 + x_hi, x_hi * 2 + c))
        greet(row_peer(-1 - x_hi, x_hi * 2 + c))
    for i in (1, 2, 3):
        greet(y_peer(i)[1])
    for i in range(1, 8):
        greet(z_peer(i)[1])

    metric_copy = pltpu.make_async_copy(metric_ref, m_f32, local_sem.at[1])
    metric_copy.start()
    own_copy = pltpu.make_async_copy(f_ref.at[0], jb.at[8, s], local_sem.at[0])
    own_copy.start()
    vir_rows = jnp.broadcast_to(vir_ref[...], (V, V))
    vir_sum[...] = vir_rows + vir_rows.T

    pl.semaphore_wait(barrier, 18)

    def remote(src, dst, send, recv, dev):
        return pltpu.make_async_remote_copy(
            src_ref=src, dst_ref=dst, send_sem=send, recv_sem=recv,
            device_id=dev, device_id_type=MESH,
        )

    def arrived(entry, q):
        remote(
            jb.at[entry, q], jb.at[entry, q], z_fwd.at[0, 0], rsem.at[entry, q], (b, mate)
        ).wait_recv()

    def slot_of(p):
        return (z + ((p + 1) // 2) * (1 - 2 * (p % 2)) + 8) % 8

    def first(i, src, dst, recv, dev):
        return remote(src, dst, init_ssem.at[i], recv, dev)

    def first_across():
        return first(0, f_ref.at[0], jb.at[8, s], rsem.at[8, s], (b, across))

    def first_mate():
        return first(1, f_ref.at[0], jb.at[8, s], rsem.at[8, s], (b, mate))

    def first_up():
        return first(2, f_ref.at[0], jb.at[z, s], rsem.at[z, s], row_peer(1, 0))

    def first_down():
        return first(3, f_ref.at[0], jb.at[z, s], rsem.at[z, s], row_peer(-1, 1))

    def chain_up():
        return first(2, f_ref.at[0], rbuf.at[1], rrsem.at[1], row_peer(2, 3))

    def chain_down():
        return first(3, f_ref.at[0], rbuf.at[0], rrsem.at[0], row_peer(-2, 3))

    def pass_on():
        return first(4, jb.at[8, across], jb.at[8, across], rsem.at[8, across], (b, mate))

    def ring_start(item, way, src, q):
        return remote(
            src, jb.at[z, q], zinit_ssem.at[item, way], rsem.at[z, q], z_peer(2 * way - 1)[1]
        )

    def ring_start_r(way):
        return remote(
            jb.at[8, across], rbuf.at[z], zinit_ssem.at[2, way], rrsem.at[z],
            z_peer(2 * way - 1)[1],
        )

    def chain_start(way):
        return remote(
            rbuf.at[1 - way], jb.at[z, 3], zinit_ssem.at[3, way], rsem.at[z, 3],
            z_peer(2 * way - 1)[1],
        )

    def ring_hop(slot, q, way):
        return remote(
            jb.at[slot, q], jb.at[slot, q], z_fwd.at[slot, q], rsem.at[slot, q],
            z_peer(2 * way - 1)[1],
        )

    def ring_hop_r(slot, way):
        return remote(
            rbuf.at[slot], rbuf.at[slot], zr_fwd.at[slot], rrsem.at[slot],
            z_peer(2 * way - 1)[1],
        )

    def to_rows(slot, src):
        return (
            remote(src, jb.at[slot, across], y_fwd.at[slot, 0], rsem.at[slot, across], row_peer(1, 0)),
            remote(src, jb.at[slot, across], y_fwd.at[slot, 1], rsem.at[slot, across], row_peer(-1, 1)),
        )

    def to_far_row(slot, q):
        up = jnp.where(slot > z, 2, -2)
        return remote(
            jb.at[slot, q], jb.at[slot, q], y_fwd.at[slot, q], rsem.at[slot, q], row_peer(up, 3)
        )

    def goes_on(p, left4):
        d = (p + 1) // 2
        return (d < 3) | ((d == 3) & (p % 2 == left4))

    first_across().start()
    first_mate().start()

    @pl.when(x_hi == 0)
    def _():
        first_up().start()
        first_down().start()

    @pl.when(s == 2)
    def _():
        for way in (1, 0):
            ring_start(2, way, f_ref.at[0], 2).start()

    @pl.when(s == 3)
    def _():
        chain_up().start()
        chain_down().start()

    own_copy.wait()
    arrived(8, across)
    pass_on().start()

    @pl.when(x_hi == 0)
    def _():
        for way in (1, 0):
            ring_start_r(way).start()
        for c in to_rows(z, jb.at[8, across]):
            c.start()
        for q in range(2):
            arrived(z, q)
            for way in (1, 0):
                ring_start(q, way, jb.at[z, q], q).start()

    @pl.when(s == 2)
    def _():
        for way in (1, 0):
            ring_start(0, way, jb.at[8, 0], 0).start()

    @pl.when(s == 3)
    def _():
        for way in (1, 0):
            remote(
                rbuf.at[0], rbuf.at[1 - way], z_fwd.at[0, 0], rrsem.at[1 - way], (b, mate)
            ).wait_recv()

        @pl.when(z < 7)
        def _():
            chain_start(1).start()

        @pl.when(z > 0)
        def _():
            chain_start(0).start()

    arrived(8, mate)

    @pl.when(s == 2)
    def _():
        for way in (1, 0):
            ring_start(3, way, jb.at[8, 3], 3).start()

    arrived(8, diag)

    @pl.when(s == 2)
    def _():
        for way in (1, 0):
            ring_start(1, way, jb.at[8, 1], 1).start()

    g_acc[...] = jnp.zeros_like(g_acc)
    dens[...] = jnp.zeros_like(dens)

    @pl.when(s == 3)
    def _():
        def chain(t, carry):
            @pl.when(z - t >= 0)
            def _():
                arrived(z - t, 3)

                @pl.when(z < 7)
                def _():
                    ring_hop(z - t, 3, 1).start()

            @pl.when(z + t < 8)
            def _():
                arrived(z + t, 3)

                @pl.when(z > 0)
                def _():
                    ring_hop(z + t, 3, 0).start()

            return carry

        lax.fori_loop(1, 8, chain, 0)

    own_e = occ_ref[b]

    def pair(entry, other):
        e_sum = own_e + occ_ref[other]
        for rc in range(V // ROWS):
            rows = pl.ds(rc * ROWS, ROWS)
            acc = dot(jb[8, 0, rows, :], jb[entry, 0], NT)
            for q in range(1, 4):
                acc = acc + dot(jb[8, q, rows, :], jb[entry, q], NT)
            t = acc / (e_sum - vir_sum[rows, :])
            t_buf[rows, :] = t
            tb_buf[rows, :] = t.astype(BF16)
        for rc in range(V // ROWS):
            rows = pl.ds(rc * ROWS, ROWS)
            ub = (2.0 * t_buf[rows, :] - t_buf[:, rows].T).astype(BF16)
            for q in range(4):
                g_acc[q, rows, :] += dot(ub, jb[entry, q], NN)
            for h in range(2):
                dens[h, rows, :] += dot(ub, tb_buf[pl.ds(h * QW, QW), :], NT)

    def relay(p, q, left4):
        slot = slot_of(p)
        arrived(slot, q)

        @pl.when(goes_on(p, left4))
        def _():
            ring_hop(slot, q, p % 2).start()

    def place(p, carry):
        slot = slot_of(p)

        @pl.when((p < 7) & (x_hi == 0))
        def _():
            nslot = slot_of(p + 1)
            remote(
                rbuf.at[0], rbuf.at[nslot], zr_fwd.at[0], rrsem.at[nslot], (b, mate)
            ).wait_recv()

            @pl.when(goes_on(p + 1, 1 - core))
            def _():
                ring_hop_r(nslot, (p + 1) % 2).start()

            for c in to_rows(nslot, rbuf.at[nslot]):
                c.start()
            relay(p + 1, 0, 1)
            relay(p + 1, 1, 0)

        @pl.when((p < 7) & (s == 2))
        def _():
            for q, left4 in ((2, 0), (0, 1), (3, 0), (1, 1)):
                relay(p + 1, q, left4)
                if q < 3:
                    to_far_row(slot_of(p + 1), q).start()

        @pl.when(x_hi == 0)
        def _():
            arrived(slot, 2)
            arrived(slot, 3)

        @pl.when((p > 0) & (s == 3))
        def _():
            for q in range(3):
                arrived(slot, q)

        shift = jnp.where(s == 0, -1, jnp.where(s == 1, 1, 0))
        shift = jnp.where(s == 3, jnp.where(slot > z, -2, 2), shift)
        other = ((b // 8 + shift + 8) % 8) * 8 + slot

        @pl.when((p > 0) | (s != 3))
        def _():
            pair(jnp.where((p == 0) & (s == 2), 8, slot), other)

        @pl.when(p == 0)
        def _():
            metric_copy.wait()
            for i in range(4):
                rows = pl.ds(i * QW, QW)
                m = m_f32[rows, :]
                hi = m.astype(BF16)
                m_hi[rows, :] = hi
                m_lo[rows, :] = (m - hi.astype(F32)).astype(BF16)

        return carry

    lax.fori_loop(0, 8, place, 0)

    sends = []

    def send(src, dst, ss, rs, dev):
        c = remote(src, dst, ss, rs, dev)
        c.start()
        sends.append(c)
        return c

    c_d0 = send(dens.at[1 - core], dr0, tail_ssem.at[0], tail_rsem.at[0], (b, mate))

    for q in range(4):
        g = g_acc[q]
        hi = g.astype(BF16)
        g_hi[q] = hi
        g_lo[q] = (g - hi.astype(F32)).astype(BF16)

    def metric_part(t):
        cols = pl.ds(pl.multiple_of(t * QW, QW), QW)
        acc = None
        for q in range(4):
            rows = pl.ds(q * QW, QW)
            mh = m_hi[rows, cols]
            ml = m_lo[rows, cols]
            term = dot(g_hi[q], mh, NN) + (dot(g_lo[q], mh, NN) + dot(g_hi[q], ml, NN))
            acc = term if acc is None else acc + term
        return acc

    part[0] = metric_part(diag)
    c_a = send(part.at[0], ra, tail_ssem.at[1], tail_rsem.at[1], (b, mate))

    c_d0.wait_recv()
    for xl in range(2):
        for yy in range(4):
            rows = pl.ds(xl * 256 + yy * 64, 64)
            d1[yy, xl] = dens[core, rows, :] + dr0[rows, :]
    y_copies = []
    for i in (1, 2, 3):
        yy, dev = y_peer(i)
        y_copies.append(send(d1.at[yy], dry.at[y], y_ssem.at[i], y_rsem.at[y], dev))

    p_across = metric_part(across)
    c_a.wait_recv()
    part[1] = p_across + ra[...]
    c_x = send(part.at[1], rx, tail_ssem.at[2], tail_rsem.at[2], (b, across))

    part[2] = metric_part(mate)
    c_b = send(part.at[2], rb, tail_ssem.at[3], tail_rsem.at[3], (b, mate))

    total = d1[y]
    for i in (1, 2, 3):
        yy, dev = y_peer(i)
        remote(d1.at[yy], dry.at[yy], y_ssem.at[i], y_rsem.at[yy], dev).wait_recv()
        total = total + dry[yy]
    for zz in range(8):
        d2[zz] = total[:, zz * 8 : zz * 8 + 8, :]
    for i in range(1, 8):
        zz, dev = z_peer(i)
        send(d2.at[zz], drz.at[z], z_ssem.at[i], z_rsem.at[z], dev)

    mine = metric_part(s)

    total = d2[z]
    for i in range(1, 8):
        zz, dev = z_peer(i)
        remote(d2.at[zz], drz.at[zz], z_ssem.at[i], z_rsem.at[zz], dev).wait_recv()
        total = total + drz[zz]
    d3[...] = total
    here = x_hi * 2 + x_lo
    for i in (1, 2, 3):
        xx, dev = x_peer(i)
        send(d3.at[xx % 2], drx.at[here], x_ssem.at[i], x_rsem.at[here], dev)
    drx[here] = d3[x_lo]

    c_b.wait_recv()
    part[3] = mine + rb[...]

    for i in (1, 2, 3):
        xx, dev = x_peer(i)
        remote(d3.at[0], drx.at[xx], x_ssem.at[i], x_rsem.at[xx], dev).wait_recv()
    d4[...] = (drx[0] + drx[1]) + (drx[2] + drx[3])
    c_4 = send(d4, dr4, tail_ssem.at[4], tail_rsem.at[4], (b, mate))
    c_4.wait_recv()

    @pl.when(core == 0)
    def _():
        dens_out_ref[:, pl.ds(0, QW)] = d4[...]
        dens_out_ref[:, pl.ds(QW, QW)] = dr4[...]

    @pl.when(core == 1)
    def _():
        dens_out_ref[:, pl.ds(0, QW)] = dr4[...]
        dens_out_ref[:, pl.ds(QW, QW)] = d4[...]

    c_x.wait_recv()
    gamma_ref[...] = (part[3] + rx[...]).T

    first_across().wait_send()
    first_mate().wait_send()
    pass_on().wait_send()

    @pl.when(x_hi == 0)
    def _():
        first_up().wait_send()
        first_down().wait_send()
        for way in (1, 0):
            ring_start_r(way).wait_send()
            for q in range(2):
                ring_start(q, way, jb.at[z, q], q).wait_send()
        for c in to_rows(z, jb.at[8, across]):
            c.wait_send()

    @pl.when(s == 2)
    def _():
        for way in (1, 0):
            for q in range(4):
                ring_start(q, way, jb.at[8, q], q).wait_send()

    @pl.when(s == 3)
    def _():
        chain_up().wait_send()
        chain_down().wait_send()

        @pl.when(z < 7)
        def _():
            chain_start(1).wait_send()

        @pl.when(z > 0)
        def _():
            chain_start(0).wait_send()

    def drain(p, carry):
        slot = slot_of(p)

        @pl.when(x_hi == 0)
        def _():
            for c in to_rows(slot, rbuf.at[slot]):
                c.wait_send()

            @pl.when(goes_on(p, 1 - core))
            def _():
                ring_hop_r(slot, p % 2).wait_send()

            for q, left4 in ((0, 1), (1, 0)):

                @pl.when(goes_on(p, left4))
                def _():
                    ring_hop(slot, q, p % 2).wait_send()

        @pl.when(s == 2)
        def _():
            for q, left4 in ((2, 0), (0, 1), (3, 0), (1, 1)):

                @pl.when(goes_on(p, left4))
                def _():
                    ring_hop(slot, q, p % 2).wait_send()

                if q < 3:
                    to_far_row(slot, q).wait_send()

        @pl.when((s == 3) & (((slot < z) & (z < 7)) | ((slot > z) & (z > 0))))
        def _():
            ring_hop(slot, 3, 0).wait_send()

        return carry

    lax.fori_loop(1, 8, drain, 0)
    for c in sends:
        c.wait_send()


def per_device(factors, occ_energy, vir_energy, metric):
    vmem = pl.BlockSpec(memory_space=pltpu.VMEM)
    dma = pltpu.SemaphoreType.DMA
    gamma, density = pl.pallas_call(
        kernel,
        out_shape=(
            jax.ShapeDtypeStruct((QW, V), F32),
            jax.ShapeDtypeStruct((8, V), F32),
        ),
        in_specs=[
            pl.BlockSpec(memory_space=pltpu.SMEM),
            vmem,
            vmem,
            pl.BlockSpec(memory_space=pl.ANY),
        ],
        out_specs=(vmem, vmem),
        scratch_shapes=[
            pltpu.VMEM((9, 4, V, QW), BF16),
            pltpu.VMEM((8, V, QW), BF16),
            pltpu.VMEM((4, V, QW), F32),
            pltpu.VMEM((2, V, QW), F32),
            pltpu.VMEM((V, V), F32),
            pltpu.VMEM((V, V), F32),
            pltpu.VMEM((V, V), BF16),
            pltpu.VMEM((4 * QW, 4 * QW), F32),
            pltpu.VMEM((4 * QW, 4 * QW), BF16),
            pltpu.VMEM((4 * QW, 4 * QW), BF16),
            pltpu.VMEM((4, V, QW), BF16),
            pltpu.VMEM((4, V, QW), BF16),
            pltpu.VMEM((4, V, QW), F32),
            pltpu.VMEM((V, QW), F32),
            pltpu.VMEM((V, QW), F32),
            pltpu.VMEM((V, QW), F32),
            pltpu.VMEM((V, QW), F32),
            pltpu.VMEM((4, 2, 64, QW), F32),
            pltpu.VMEM((4, 2, 64, QW), F32),
            pltpu.VMEM((8, 2, 8, QW), F32),
            pltpu.VMEM((8, 2, 8, QW), F32),
            pltpu.VMEM((2, 8, QW), F32),
            pltpu.VMEM((4, 8, QW), F32),
            pltpu.VMEM((8, QW), F32),
            pltpu.VMEM((8, QW), F32),
            dma((2,)),
            dma((5,)),
            dma((4, 2)),
            dma((8, 4)),
            dma((8,)),
            dma((8, 4)),
            dma((9, 4)),
            dma((8,)),
            dma((5,)),
            dma((5,)),
            dma((4,)),
            dma((4,)),
            dma((8,)),
            dma((8,)),
            dma((4,)),
            dma((4,)),
        ],
        compiler_params=pltpu.CompilerParams(
            collective_id=0, has_side_effects=True, vmem_limit_bytes=60 * 1024 * 1024
        ),
    )(occ_energy, factors, vir_energy.reshape(1, V), metric)
    return gamma.reshape(QW, 1, V), density


def solution(mesh):
    return jax.shard_map(
        per_device,
        mesh=mesh,
        in_specs=(P("blk", None, "sec"), P(), P(), P()),
        out_specs=(P("sec", "blk", None), P("blk", None)),
        check_vma=False,
    )
```

```python
import jax
import jax.numpy as jnp
from jax import lax
from jax.experimental import pallas as pl
from jax.experimental.pallas import tpu as pltpu
from jax.sharding import PartitionSpec as P

MESH = pl.DeviceIdType.MESH
F32 = jnp.float32
BF16 = jnp.bfloat16
NT = (((1,), (1,)), ((), ()))
NN = (((1,), (0,)), ((), ()))

V = 512
QW = 256
NB = 64
ROWS = 256


def dot(a, b, dims):
    return lax.dot_general(a, b, dims, preferred_element_type=F32)


def kernel(
    occ_ref,
    f_ref,
    vir_ref,
    metric_ref,
    gamma_ref,
    dens_out_ref,
    jb,
    rbuf,
    g_acc,
    dens,
    vir_sum,
    t_buf,
    tb_buf,
    m_f32,
    m_hi,
    m_lo,
    g_hi,
    g_lo,
    part,
    ra,
    rb,
    rx,
    dr0,
    d1,
    dry,
    d2,
    drz,
    d3,
    drx,
    occ_sm,
    vir_vm,
    local_sem,
    init_ssem,
    zinit_ssem,
    z_fwd,
    zr_fwd,
    y_fwd,
    rsem,
    rrsem,
    tail_ssem,
    tail_rsem,
    half_ssem,
    half_rsem,
    y_ssem,
    y_rsem,
    z_ssem,
    z_rsem,
    x_ssem,
    x_rsem,
):
    b = lax.axis_index("blk")
    s = lax.axis_index("sec")
    x_hi = s // 2
    core = s % 2
    x_lo = b // 32
    y = (b // 8) % 4
    z = b % 8
    mate = s + 1 - 2 * core
    across = (s + 2) % 4
    diag = 3 - s

    def y_peer(i):
        yy = (y + i) % 4
        return yy, (x_lo * 32 + yy * 8 + z, s)

    def z_peer(i):
        zz = (z + i + 8) % 8
        return zz, (x_lo * 32 + y * 8 + zz, s)

    def x_peer(i, to_core):
        xx = (x_hi * 2 + x_lo + i) % 4
        return xx, ((xx % 2) * 32 + y * 8 + z, (xx // 2) * 2 + to_core)

    def row_peer(rows, sec):
        return ((b + 8 * rows + NB) % NB, sec)

    barrier = pltpu.get_barrier_semaphore()

    def greet(dev):
        pl.semaphore_signal(barrier, inc=1, device_id=dev, device_id_type=MESH)

    occ_copy = pltpu.make_async_copy(occ_ref, occ_sm, local_sem.at[2])
    vir_copy = pltpu.make_async_copy(vir_ref, vir_vm, local_sem.at[3])
    metric_copy = pltpu.make_async_copy(metric_ref, m_f32, local_sem.at[1])
    own_copy = pltpu.make_async_copy(f_ref.at[0], jb.at[8, s], local_sem.at[0])

    greet((b, mate))
    for i in (1, 2, 3):
        for c in range(2):
            greet(x_peer(i, c)[1])
    for c in range(2):
        greet(row_peer(1 + x_hi, x_hi * 2 + c))
        greet(row_peer(-1 - x_hi, x_hi * 2 + c))
    for i in (1, 2, 3):
        greet(y_peer(i)[1])
    for i in range(1, 8):
        greet(z_peer(i)[1])

    vir_copy.start()
    occ_copy.start()
    own_copy.start()
    metric_copy.start()
    vir_copy.wait()
    vir_rows = jnp.broadcast_to(vir_vm[...], (V, V))
    vir_sum[...] = vir_rows + vir_rows.T
    g_acc[...] = jnp.zeros_like(g_acc)
    dens[...] = jnp.zeros_like(dens)

    pl.semaphore_wait(barrier, 21)

    def remote(src, dst, send, recv, dev):
        return pltpu.make_async_remote_copy(
            src_ref=src, dst_ref=dst, send_sem=send, recv_sem=recv,
            device_id=dev, device_id_type=MESH,
        )

    def arrived(entry, q):
        remote(
            jb.at[entry, q], jb.at[entry, q], z_fwd.at[0, 0], rsem.at[entry, q], (b, mate)
        ).wait_recv()

    def slot_of(p):
        return (z + ((p + 1) // 2) * (1 - 2 * (p % 2)) + 8) % 8

    def first(i, src, dst, recv, dev):
        return remote(src, dst, init_ssem.at[i], recv, dev)

    def first_across():
        return first(0, f_ref.at[0], jb.at[8, s], rsem.at[8, s], (b, across))

    def first_mate():
        return first(1, f_ref.at[0], jb.at[8, s], rsem.at[8, s], (b, mate))

    def first_up():
        return first(
            2, jb.at[8, across], jb.at[z, across], rsem.at[z, across], row_peer(1, 0)
        )

    def first_down():
        return first(
            3, jb.at[8, across], jb.at[z, across], rsem.at[z, across], row_peer(-1, 1)
        )

    def chain_up():
        return first(2, f_ref.at[0], rbuf.at[1], rrsem.at[1], row_peer(2, 3))

    def chain_down():
        return first(3, f_ref.at[0], rbuf.at[0], rrsem.at[0], row_peer(-2, 3))

    def pass_on():
        return first(4, jb.at[8, across], jb.at[8, across], rsem.at[8, across], (b, mate))

    def ring_start(item, way, src, q):
        return remote(
            src, jb.at[z, q], zinit_ssem.at[item, way], rsem.at[z, q], z_peer(2 * way - 1)[1]
        )

    def ring_start_r(way):
        return remote(
            f_ref.at[0], rbuf.at[z], zinit_ssem.at[0, way], rrsem.at[z], z_peer(2 * way - 1)[1]
        )

    def chain_start(way):
        return remote(
            rbuf.at[1 - way], jb.at[z, 3], zinit_ssem.at[3, way], rsem.at[z, 3],
            z_peer(2 * way - 1)[1],
        )

    def ring_hop(slot, q, way):
        return remote(
            jb.at[slot, q], jb.at[slot, q], z_fwd.at[slot, q], rsem.at[slot, q],
            z_peer(2 * way - 1)[1],
        )

    def ring_hop_r(slot, way):
        return remote(
            rbuf.at[slot], rbuf.at[slot], zr_fwd.at[slot], rrsem.at[slot],
            z_peer(2 * way - 1)[1],
        )

    def to_rows(slot, src):
        return (
            remote(src, jb.at[slot, s], y_fwd.at[slot, 0], rsem.at[slot, s], row_peer(1, 0)),
            remote(src, jb.at[slot, s], y_fwd.at[slot, 1], rsem.at[slot, s], row_peer(-1, 1)),
        )

    def to_far_row(slot, q):
        up = jnp.where(slot > z, 2, -2)
        return remote(
            jb.at[slot, q], jb.at[slot, q], y_fwd.at[slot, q], rsem.at[slot, q], row_peer(up, 3)
        )

    def goes_on(p, left4):
        d = (p + 1) // 2
        return (d < 3) | ((d == 3) & (p % 2 == left4))

    def relay(p, q, left4):
        slot = slot_of(p)
        arrived(slot, q)

        @pl.when(goes_on(p, left4))
        def _():
            ring_hop(slot, q, p % 2).start()

    def relay_r(p):
        slot = slot_of(p)
        remote(
            rbuf.at[0], rbuf.at[slot], zr_fwd.at[0], rrsem.at[slot], (b, mate)
        ).wait_recv()

        @pl.when(goes_on(p, 1 - core))
        def _():
            ring_hop_r(slot, p % 2).start()

        for c in to_rows(slot, rbuf.at[slot]):
            c.start()

    @pl.when(s == 2)
    def _():
        for way in (1, 0):
            ring_start(2, way, f_ref.at[0], 2).start()

    @pl.when(x_hi == 0)
    def _():
        for way in (1, 0):
            ring_start_r(way).start()

    first_across().start()
    first_mate().start()

    @pl.when(x_hi == 0)
    def _():
        for c in to_rows(z, f_ref.at[0]):
            c.start()

    @pl.when(s == 3)
    def _():
        chain_up().start()
        chain_down().start()

    occ_copy.wait()
    own_copy.wait()
    metric_copy.wait()
    for i in range(4):
        rows = pl.ds(i * QW, QW)
        m = m_f32[rows, :]
        hi = m.astype(BF16)
        m_hi[rows, :] = hi
        m_lo[rows, :] = (m - hi.astype(F32)).astype(BF16)

    arrived(8, mate)

    @pl.when(x_hi == 0)
    def _():
        for p in (1, 2):
            relay_r(p)

    @pl.when(s == 2)
    def _():
        for way in (1, 0):
            ring_start(3, way, jb.at[8, 3], 3).start()
        for p in (1, 2):
            relay(p, 2, 0)
            to_far_row(slot_of(p), 2).start()

    arrived(8, across)
    pass_on().start()

    @pl.when(x_hi == 0)
    def _():
        first_up().start()
        first_down().start()
        for p in (3, 4):
            relay_r(p)

    @pl.when(s == 2)
    def _():
        for way in (1, 0):
            ring_start(0, way, jb.at[8, 0], 0).start()

    arrived(8, diag)

    @pl.when(s == 2)
    def _():
        for way in (1, 0):
            ring_start(1, way, jb.at[8, 1], 1).start()

    @pl.when(s == 3)
    def _():
        for way in (1, 0):
            remote(
                rbuf.at[0], rbuf.at[1 - way], z_fwd.at[0, 0], rrsem.at[1 - way], (b, mate)
            ).wait_recv()

        @pl.when(z < 7)
        def _():
            chain_start(1).start()

        @pl.when(z > 0)
        def _():
            chain_start(0).start()

        def chain(t, carry):
            @pl.when(z - t >= 0)
            def _():
                arrived(z - t, 3)

                @pl.when(z < 7)
                def _():
                    ring_hop(z - t, 3, 1).start()

            @pl.when(z + t < 8)
            def _():
                arrived(z + t, 3)

                @pl.when(z > 0)
                def _():
                    ring_hop(z + t, 3, 0).start()

            return carry

        lax.fori_loop(1, 8, chain, 0)

    own_e = occ_sm[b]

    def pair(entry, other):
        e_sum = own_e + occ_sm[other]
        for rc in range(V // ROWS):
            rows = pl.ds(rc * ROWS, ROWS)
            acc = dot(jb[8, 0, rows, :], jb[entry, 0], NT)
            for q in range(1, 4):
                acc = acc + dot(jb[8, q, rows, :], jb[entry, q], NT)
            t = acc / (e_sum - vir_sum[rows, :])
            t_buf[rows, :] = t
            tb_buf[rows, :] = t.astype(BF16)
        for rc in range(V // ROWS):
            rows = pl.ds(rc * ROWS, ROWS)
            ub = (2.0 * t_buf[rows, :] - t_buf[:, rows].T).astype(BF16)
            for q in range(4):
                g_acc[q, rows, :] += dot(ub, jb[entry, q], NN)
            for h in range(2):
                dens[h, rows, :] += dot(ub, tb_buf[pl.ds(h * QW, QW), :], NT)

    def place(p, carry):
        slot = slot_of(p)

        @pl.when((p == 0) & (x_hi == 0))
        def _():
            for q in (2, 3):
                arrived(z, q)
                for way in (1, 0):
                    ring_start(q, way, jb.at[z, q], q).start()
            for n in (5, 6):
                relay_r(n)

        @pl.when((p == 1) & (x_hi == 0))
        def _():
            relay_r(7)

        @pl.when((p > 0) & (x_hi == 0))
        def _():
            relay(p, 2, 1)
            relay(p, 3, 0)

        @pl.when((p < 5) & (s == 2))
        def _():
            relay(p + 3, 2, 0)
            to_far_row(slot_of(p + 3), 2).start()

        @pl.when((p > 0) & (s == 2))
        def _():
            relay(p, 3, 0)
            for q in (0, 1):
                relay(p, q, 1)
                to_far_row(slot, q).start()

        @pl.when(x_hi == 0)
        def _():
            arrived(slot, 0)
            arrived(slot, 1)

        @pl.when((p > 0) & (s == 3))
        def _():
            for q in (2, 0, 1):
                arrived(slot, q)

        shift = jnp.where(s == 0, -1, jnp.where(s == 1, 1, 0))
        shift = jnp.where(s == 3, jnp.where(slot > z, -2, 2), shift)
        other = ((b // 8 + shift + 8) % 8) * 8 + slot

        @pl.when((p > 0) | (s != 3))
        def _():
            pair(jnp.where((p == 0) & (s == 2), 8, slot), other)

        return carry

    lax.fori_loop(0, 8, place, 0)

    sends = []

    def send(src, dst, ss, rs, dev):
        c = remote(src, dst, ss, rs, dev)
        c.start()
        sends.append(c)
        return c

    c_d0 = send(dens.at[1 - core], dr0, tail_ssem.at[0], tail_rsem.at[0], (b, mate))

    for q in range(4):
        g = g_acc[q]
        hi = g.astype(BF16)
        g_hi[q] = hi
        g_lo[q] = (g - hi.astype(F32)).astype(BF16)

    def metric_part(t, rows):
        cols = pl.ds(pl.multiple_of(t * QW, QW), QW)
        acc = None
        for q in range(4):
            depth = pl.ds(q * QW, QW)
            mh = m_hi[depth, cols]
            ml = m_lo[depth, cols]
            gh = g_hi[q, rows, :]
            term = dot(gh, mh, NN) + (dot(g_lo[q, rows, :], mh, NN) + dot(gh, ml, NN))
            acc = term if acc is None else acc + term
        return acc

    halves = [pl.ds(h * QW, QW) for h in range(2)]
    everything = pl.ds(0, V)
    to_mate = []
    for h, rows in enumerate(halves):
        part[0, rows, :] = metric_part(diag, rows)
        to_mate.append(
            send(
                part.at[0, rows], ra.at[rows], half_ssem.at[0, h], half_rsem.at[0, h], (b, mate)
            )
        )

    c_d0.wait_recv()
    for xl in range(2):
        for yy in range(4):
            rows = pl.ds(xl * 256 + yy * 64, 64)
            d1[yy, xl] = dens[core, rows, :] + dr0[rows, :]
    for i in (1, 2, 3):
        yy, dev = y_peer(i)
        send(d1.at[yy], dry.at[y], y_ssem.at[i], y_rsem.at[y], dev)

    to_across = []
    for h, rows in enumerate(halves):
        p_across = metric_part(across, rows)
        to_mate[h].wait_recv()
        part[1, rows, :] = p_across + ra[rows, :]
        to_across.append(
            send(
                part.at[1, rows], rx.at[rows], half_ssem.at[1, h], half_rsem.at[1, h], (b, across)
            )
        )

    part[2] = metric_part(mate, everything)
    c_b = send(part.at[2], rb, tail_ssem.at[1], tail_rsem.at[1], (b, mate))

    total = d1[y]
    for i in (1, 2, 3):
        yy, dev = y_peer(i)
        remote(d1.at[yy], dry.at[yy], y_ssem.at[i], y_rsem.at[yy], dev).wait_recv()
        total = total + dry[yy]
    for zz in range(8):
        d2[zz] = total[:, zz * 8 : zz * 8 + 8, :]
    for i in range(1, 8):
        zz, dev = z_peer(i)
        send(d2.at[zz], drz.at[z], z_ssem.at[i], z_rsem.at[z], dev)

    part[3] = metric_part(s, everything)

    total = d2[z]
    for i in range(1, 8):
        zz, dev = z_peer(i)
        remote(d2.at[zz], drz.at[zz], z_ssem.at[i], z_rsem.at[zz], dev).wait_recv()
        total = total + drz[zz]
    d3[...] = total
    here = x_hi * 2 + x_lo
    drx[core, here] = d3[x_lo]
    send(d3.at[x_lo], drx.at[core, here], tail_ssem.at[2], x_rsem.at[core, here], (b, mate))
    for i in (1, 2, 3):
        for c in range(2):
            xx, dev = x_peer(i, c)
            send(
                d3.at[xx % 2], drx.at[core, here], x_ssem.at[c, i], x_rsem.at[core, here], dev
            )

    c_b.wait_recv()
    part[3] = part[3] + rb[...]

    def dens_arrived(c, xx):
        remote(
            d3.at[0], drx.at[c, xx], x_ssem.at[0, 0], x_rsem.at[c, xx], (b, mate)
        ).wait_recv()

    dens_arrived(1 - core, here)
    for i in (1, 2, 3):
        for c in range(2):
            dens_arrived(c, x_peer(i, c)[0])
    for c in range(2):
        dens_out_ref[:, pl.ds(c * QW, QW)] = (drx[c, 0] + drx[c, 1]) + (drx[c, 2] + drx[c, 3])

    for h, rows in enumerate(halves):
        to_across[h].wait_recv()
        done = (part[3, rows, :] + rx[rows, :]).T
        for j in range(2):
            gamma_ref[pl.ds(2 * h + j, QW, stride=4), :] = done[:, j * 128 : j * 128 + 128]

    first_across().wait_send()
    first_mate().wait_send()
    pass_on().wait_send()

    @pl.when(x_hi == 0)
    def _():
        first_up().wait_send()
        first_down().wait_send()
        for way in (1, 0):
            ring_start_r(way).wait_send()
            for q in (2, 3):
                ring_start(q, way, jb.at[z, q], q).wait_send()
        for c in to_rows(z, f_ref.at[0]):
            c.wait_send()

    @pl.when(s == 2)
    def _():
        for way in (1, 0):
            for q in range(4):
                ring_start(q, way, jb.at[8, q], q).wait_send()

    @pl.when(s == 3)
    def _():
        chain_up().wait_send()
        chain_down().wait_send()

        @pl.when(z < 7)
        def _():
            chain_start(1).wait_send()

        @pl.when(z > 0)
        def _():
            chain_start(0).wait_send()

    def drain(p, carry):
        slot = slot_of(p)

        @pl.when(x_hi == 0)
        def _():
            for c in to_rows(slot, rbuf.at[slot]):
                c.wait_send()

            @pl.when(goes_on(p, 1 - core))
            def _():
                ring_hop_r(slot, p % 2).wait_send()

            for q, left4 in ((2, 1), (3, 0)):

                @pl.when(goes_on(p, left4))
                def _():
                    ring_hop(slot, q, p % 2).wait_send()

        @pl.when(s == 2)
        def _():
            for q, left4 in ((2, 0), (0, 1), (3, 0), (1, 1)):

                @pl.when(goes_on(p, left4))
                def _():
                    ring_hop(slot, q, p % 2).wait_send()

                if q < 3:
                    to_far_row(slot, q).wait_send()

        @pl.when((s == 3) & (((slot < z) & (z < 7)) | ((slot > z) & (z > 0))))
        def _():
            ring_hop(slot, 3, 0).wait_send()

        return carry

    lax.fori_loop(1, 8, drain, 0)
    for c in sends:
        c.wait_send()


def hand_over(gamma_ref, dens_ref, gamma_out, dens_out):
    gamma_out[...] = gamma_ref[...]
    dens_out[...] = dens_ref[...]


def per_device(factors, occ_energy, vir_energy, metric):
    vmem = pl.BlockSpec(memory_space=pltpu.VMEM)
    hbm = pl.BlockSpec(memory_space=pltpu.HBM)
    dma = pltpu.SemaphoreType.DMA
    outs = (
        jax.ShapeDtypeStruct((4 * QW, 128), F32),
        jax.ShapeDtypeStruct((8, V), F32),
    )
    gamma, density = pl.pallas_call(
        kernel,
        out_shape=outs,
        in_specs=[hbm, hbm, hbm, hbm],
        out_specs=(vmem, vmem),
        scratch_shapes=[
            pltpu.VMEM((9, 4, V, QW), BF16),
            pltpu.VMEM((8, V, QW), BF16),
            pltpu.VMEM((4, V, QW), F32),
            pltpu.VMEM((2, V, QW), F32),
            pltpu.VMEM((V, V), F32),
            pltpu.VMEM((V, V), F32),
            pltpu.VMEM((V, V), BF16),
            pltpu.VMEM((4 * QW, 4 * QW), F32),
            pltpu.VMEM((4 * QW, 4 * QW), BF16),
            pltpu.VMEM((4 * QW, 4 * QW), BF16),
            pltpu.VMEM((4, V, QW), BF16),
            pltpu.VMEM((4, V, QW), BF16),
            pltpu.VMEM((4, V, QW), F32),
            pltpu.VMEM((V, QW), F32),
            pltpu.VMEM((V, QW), F32),
            pltpu.VMEM((V, QW), F32),
            pltpu.VMEM((V, QW), F32),
            pltpu.VMEM((4, 2, 64, QW), F32),
            pltpu.VMEM((4, 2, 64, QW), F32),
            pltpu.VMEM((8, 2, 8, QW), F32),
            pltpu.VMEM((8, 2, 8, QW), F32),
            pltpu.VMEM((2, 8, QW), F32),
            pltpu.VMEM((2, 4, 8, QW), F32),
            pltpu.SMEM((NB,), F32),
            pltpu.VMEM((1, V), F32),
            dma((4,)),
            dma((5,)),
            dma((4, 2)),
            dma((8, 4)),
            dma((8,)),
            dma((8, 4)),
            dma((9, 4)),
            dma((8,)),
            dma((3,)),
            dma((3,)),
            dma((2, 2)),
            dma((2, 2)),
            dma((4,)),
            dma((4,)),
            dma((8,)),
            dma((8,)),
            dma((2, 4)),
            dma((2, 4)),
        ],
        compiler_params=pltpu.CompilerParams(
            collective_id=0, has_side_effects=True, vmem_limit_bytes=60 * 1024 * 1024
        ),
    )(occ_energy, factors, vir_energy.reshape(1, V), metric)
    gamma, density = pl.pallas_call(
        hand_over,
        out_shape=outs,
        in_specs=[vmem, vmem],
        out_specs=(vmem, vmem),
        compiler_params=pltpu.CompilerParams(vmem_limit_bytes=4 * 1024 * 1024),
    )(gamma, density)
    return gamma.reshape(QW, 1, V), density


def solution(mesh):
    return jax.shard_map(
        per_device,
        mesh=mesh,
        in_specs=(P("blk", None, "sec"), P(), P(), P()),
        out_specs=(P("sec", "blk", None), P("blk", None)),
        check_vma=False,
    )
```

```python
import jax
import jax.numpy as jnp
from jax import lax
from jax.experimental import pallas as pl
from jax.experimental.pallas import tpu as pltpu
from jax.sharding import PartitionSpec as P

MESH = pl.DeviceIdType.MESH
F32 = jnp.float32
BF16 = jnp.bfloat16
NT = (((1,), (1,)), ((), ()))
NN = (((1,), (0,)), ((), ()))

V = 512
QW = 256
NB = 64
ROWS = 256


def dot(a, b, dims):
    return lax.dot_general(a, b, dims, preferred_element_type=F32)


def kernel(
    occ_ref,
    f_ref,
    vir_ref,
    metric_ref,
    out_ref,
    jb,
    rbuf,
    g_acc,
    dens,
    vir_sum,
    t_buf,
    tb_buf,
    m_f32,
    m_hi,
    m_lo,
    g_hi,
    g_lo,
    part,
    ra,
    rb,
    rx,
    dr0,
    d1,
    dry,
    d2,
    drz,
    d3,
    drx,
    occ_sm,
    vir_vm,
    local_sem,
    init_ssem,
    zinit_ssem,
    z_fwd,
    zr_fwd,
    y_fwd,
    rsem,
    rrsem,
    tail_ssem,
    tail_rsem,
    half_ssem,
    half_rsem,
    y_ssem,
    y_rsem,
    z_ssem,
    z_rsem,
    x_ssem,
    x_rsem,
):
    b = lax.axis_index("blk")
    s = lax.axis_index("sec")
    x_hi = s // 2
    core = s % 2
    x_lo = b // 32
    y = (b // 8) % 4
    z = b % 8
    mate = s + 1 - 2 * core
    across = (s + 2) % 4
    diag = 3 - s

    def y_peer(i):
        yy = (y + i) % 4
        return yy, (x_lo * 32 + yy * 8 + z, s)

    def z_peer(i):
        zz = (z + i + 8) % 8
        return zz, (x_lo * 32 + y * 8 + zz, s)

    def x_peer(i, to_core):
        xx = (x_hi * 2 + x_lo + i) % 4
        return xx, ((xx % 2) * 32 + y * 8 + z, (xx // 2) * 2 + to_core)

    def row_peer(rows, sec):
        return ((b + 8 * rows + NB) % NB, sec)

    barrier = pltpu.get_barrier_semaphore()

    def greet(dev):
        pl.semaphore_signal(barrier, inc=1, device_id=dev, device_id_type=MESH)

    occ_copy = pltpu.make_async_copy(occ_ref, occ_sm, local_sem.at[2])
    vir_copy = pltpu.make_async_copy(vir_ref, vir_vm, local_sem.at[3])
    metric_copy = pltpu.make_async_copy(metric_ref, m_f32, local_sem.at[1])
    own_copy = pltpu.make_async_copy(f_ref.at[0], jb.at[8, s], local_sem.at[0])

    greet((b, mate))
    for i in (1, 2, 3):
        for c in range(2):
            greet(x_peer(i, c)[1])
    for c in range(2):
        greet(row_peer(1 + x_hi, x_hi * 2 + c))
        greet(row_peer(-1 - x_hi, x_hi * 2 + c))
    for i in (1, 2, 3):
        greet(y_peer(i)[1])
    for i in range(1, 8):
        greet(z_peer(i)[1])

    vir_copy.start()
    occ_copy.start()
    own_copy.start()
    metric_copy.start()
    vir_copy.wait()
    vir_rows = jnp.broadcast_to(vir_vm[...], (V, V))
    vir_sum[...] = vir_rows + vir_rows.T
    g_acc[...] = jnp.zeros_like(g_acc)
    dens[...] = jnp.zeros_like(dens)

    pl.semaphore_wait(barrier, 21)

    def remote(src, dst, send, recv, dev):
        return pltpu.make_async_remote_copy(
            src_ref=src, dst_ref=dst, send_sem=send, recv_sem=recv,
            device_id=dev, device_id_type=MESH,
        )

    def arrived(entry, q):
        remote(
            jb.at[entry, q], jb.at[entry, q], z_fwd.at[0, 0], rsem.at[entry, q], (b, mate)
        ).wait_recv()

    def slot_of(p):
        return (z + ((p + 1) // 2) * (1 - 2 * (p % 2)) + 8) % 8

    def first(i, src, dst, recv, dev):
        return remote(src, dst, init_ssem.at[i], recv, dev)

    def first_across():
        return first(0, f_ref.at[0], jb.at[8, s], rsem.at[8, s], (b, across))

    def first_mate():
        return first(1, f_ref.at[0], jb.at[8, s], rsem.at[8, s], (b, mate))

    def first_up():
        return first(
            2, jb.at[8, across], jb.at[z, across], rsem.at[z, across], row_peer(1, 0)
        )

    def first_down():
        return first(
            3, jb.at[8, across], jb.at[z, across], rsem.at[z, across], row_peer(-1, 1)
        )

    def chain_up():
        return first(2, f_ref.at[0], rbuf.at[1], rrsem.at[1, 0], row_peer(2, 3))

    def chain_down():
        return first(3, f_ref.at[0], rbuf.at[0], rrsem.at[0, 0], row_peer(-2, 3))

    def pass_on():
        return first(4, jb.at[8, across], jb.at[8, across], rsem.at[8, across], (b, mate))

    def ring_start(item, way, src, q):
        return remote(
            src, jb.at[z, q], zinit_ssem.at[item, way], rsem.at[z, q], z_peer(2 * way - 1)[1]
        )

    halves = [pl.ds(h * QW, QW) for h in range(2)]

    def ring_start_r(way, h):
        return remote(
            f_ref.at[0, halves[h]], rbuf.at[z, halves[h]], zinit_ssem.at[h, way],
            rrsem.at[z, h], z_peer(2 * way - 1)[1],
        )

    def chain_start(way):
        return remote(
            rbuf.at[1 - way], jb.at[z, 3], zinit_ssem.at[3, way], rsem.at[z, 3],
            z_peer(2 * way - 1)[1],
        )

    def ring_hop(slot, q, way):
        return remote(
            jb.at[slot, q], jb.at[slot, q], z_fwd.at[slot, q], rsem.at[slot, q],
            z_peer(2 * way - 1)[1],
        )

    def ring_hop_r(slot, way, h):
        return remote(
            rbuf.at[slot, halves[h]], rbuf.at[slot, halves[h]], zr_fwd.at[slot, h],
            rrsem.at[slot, h], z_peer(2 * way - 1)[1],
        )

    def to_rows(slot, src):
        return (
            remote(src, jb.at[slot, s], y_fwd.at[slot, 0], rsem.at[slot, s], row_peer(1, 0)),
            remote(src, jb.at[slot, s], y_fwd.at[slot, 1], rsem.at[slot, s], row_peer(-1, 1)),
        )

    def to_far_row(slot, q):
        up = jnp.where(slot > z, 2, -2)
        return remote(
            jb.at[slot, q], jb.at[slot, q], y_fwd.at[slot, q], rsem.at[slot, q], row_peer(up, 3)
        )

    def goes_on(p, left4):
        d = (p + 1) // 2
        return (d < 3) | ((d == 3) & (p % 2 == left4))

    def relay(p, q, left4):
        slot = slot_of(p)
        arrived(slot, q)

        @pl.when(goes_on(p, left4))
        def _():
            ring_hop(slot, q, p % 2).start()

    def relay_r(p):
        slot = slot_of(p)
        for h in range(2):
            ring_hop_r(slot, 0, h).wait_recv()

            @pl.when(goes_on(p, 1 - core))
            def _():
                ring_hop_r(slot, p % 2, h).start()

    def rows_r(p):
        slot = slot_of(p)
        for c in to_rows(slot, rbuf.at[slot]):
            c.start()

    @pl.when(s == 2)
    def _():
        for way in (1, 0):
            ring_start(2, way, f_ref.at[0], 2).start()

    @pl.when(x_hi == 0)
    def _():
        for h in range(2):
            for way in (1, 0):
                ring_start_r(way, h).start()

    first_across().start()
    first_mate().start()

    @pl.when(x_hi == 0)
    def _():
        for c in to_rows(z, f_ref.at[0]):
            c.start()

    @pl.when(s == 3)
    def _():
        chain_up().start()
        chain_down().start()

    occ_copy.wait()
    own_copy.wait()
    metric_copy.wait()
    for i in range(4):
        rows = pl.ds(i * QW, QW)
        m = m_f32[rows, :]
        hi = m.astype(BF16)
        m_hi[rows, :] = hi
        m_lo[rows, :] = (m - hi.astype(F32)).astype(BF16)

    arrived(8, mate)

    @pl.when(x_hi == 0)
    def _():
        for p in (1, 2):
            relay_r(p)

    @pl.when(s == 2)
    def _():
        for p in (1, 2):
            relay(p, 2, 0)
            to_far_row(slot_of(p), 2).start()

    arrived(8, across)
    pass_on().start()

    @pl.when(x_hi == 0)
    def _():
        first_up().start()
        first_down().start()
        for p in (1, 2):
            rows_r(p)
        for p in (3, 4):
            relay_r(p)
            rows_r(p)

    @pl.when(s == 2)
    def _():
        for way in (1, 0):
            ring_start(0, way, jb.at[8, 0], 0).start()

    arrived(8, diag)

    @pl.when(s == 2)
    def _():
        for q in (1, 3):
            for way in (1, 0):
                ring_start(q, way, jb.at[8, q], q).start()

    @pl.when(s == 3)
    def _():
        for way in (1, 0):
            remote(
                rbuf.at[0], rbuf.at[1 - way], z_fwd.at[0, 0], rrsem.at[1 - way, 0], (b, mate)
            ).wait_recv()

        @pl.when(z < 7)
        def _():
            chain_start(1).start()

        @pl.when(z > 0)
        def _():
            chain_start(0).start()

        def chain(t, carry):
            @pl.when(z - t >= 0)
            def _():
                arrived(z - t, 3)

                @pl.when(z < 7)
                def _():
                    ring_hop(z - t, 3, 1).start()

            @pl.when(z + t < 8)
            def _():
                arrived(z + t, 3)

                @pl.when(z > 0)
                def _():
                    ring_hop(z + t, 3, 0).start()

            return carry

        lax.fori_loop(1, 8, chain, 0)

    own_e = occ_sm[b]

    def pair(entry, other):
        e_sum = own_e + occ_sm[other]
        for rc in range(V // ROWS):
            rows = pl.ds(rc * ROWS, ROWS)
            acc = dot(jb[8, 0, rows, :], jb[entry, 0], NT)
            for q in range(1, 4):
                acc = acc + dot(jb[8, q, rows, :], jb[entry, q], NT)
            t = acc / (e_sum - vir_sum[rows, :])
            t_buf[rows, :] = t
            tb_buf[rows, :] = t.astype(BF16)
        for rc in range(V // ROWS):
            rows = pl.ds(rc * ROWS, ROWS)
            ub = (2.0 * t_buf[rows, :] - t_buf[:, rows].T).astype(BF16)
            for h in range(2):
                dens[h, rows, :] += dot(ub, tb_buf[pl.ds(h * QW, QW), :], NT)
            for q in range(4):
                g_acc[q, rows, :] += dot(ub, jb[entry, q], NN)

    def place(p, carry):
        slot = slot_of(p)

        @pl.when((p == 0) & (x_hi == 0))
        def _():
            for q in (2, 3):
                arrived(z, q)
                for way in (1, 0):
                    ring_start(q, way, jb.at[z, q], q).start()
            for n in (5, 6):
                relay_r(n)
                rows_r(n)

        @pl.when((p == 1) & (x_hi == 0))
        def _():
            relay_r(7)
            rows_r(7)

        @pl.when((p > 0) & (x_hi == 0))
        def _():
            relay(p, 2, 1)
            relay(p, 3, 0)

        @pl.when((p < 5) & (s == 2))
        def _():
            relay(p + 3, 2, 0)
            to_far_row(slot_of(p + 3), 2).start()

        @pl.when((p < 7) & (s == 2))
        def _():
            for q in (0, 1):
                relay(p + 1, q, 1)
                to_far_row(slot_of(p + 1), q).start()

        @pl.when((p > 0) & (s == 2))
        def _():
            relay(p, 3, 0)

        @pl.when(x_hi == 0)
        def _():
            arrived(slot, 0)
            arrived(slot, 1)

        @pl.when((p > 0) & (s == 3))
        def _():
            for q in (2, 0, 1):
                arrived(slot, q)

        shift = jnp.where(s == 0, -1, jnp.where(s == 1, 1, 0))
        shift = jnp.where(s == 3, jnp.where(slot > z, -2, 2), shift)
        other = ((b // 8 + shift + 8) % 8) * 8 + slot

        @pl.when((p > 0) | (s != 3))
        def _():
            pair(jnp.where((p == 0) & (s == 2), 8, slot), other)

        return carry

    lax.fori_loop(0, 8, place, 0)

    sends = []

    def send(src, dst, ss, rs, dev):
        c = remote(src, dst, ss, rs, dev)
        c.start()
        sends.append(c)
        return c

    c_d0 = send(dens.at[1 - core], dr0, tail_ssem.at[0], tail_rsem.at[0], (b, mate))

    for q in range(4):
        g = g_acc[q]
        hi = g.astype(BF16)
        g_hi[q] = hi
        g_lo[q] = (g - hi.astype(F32)).astype(BF16)

    def metric_part(t, rows):
        cols = pl.ds(pl.multiple_of(t * QW, QW), QW)
        acc = None
        for q in range(4):
            depth = pl.ds(q * QW, QW)
            mh = m_hi[depth, cols]
            ml = m_lo[depth, cols]
            gh = g_hi[q, rows, :]
            term = dot(gh, mh, NN) + (dot(g_lo[q, rows, :], mh, NN) + dot(gh, ml, NN))
            acc = term if acc is None else acc + term
        return acc

    everything = pl.ds(0, V)
    to_mate = []

    def first_product(h):
        rows = halves[h]
        part[0, rows, :] = metric_part(diag, rows)
        to_mate.append(
            send(
                part.at[0, rows], ra.at[rows], half_ssem.at[0, h], half_rsem.at[0, h], (b, mate)
            )
        )

    first_product(0)
    c_d0.wait_recv()
    for yy in range(4):
        for xl in range(2):
            rows = pl.ds(xl * 256 + yy * 64, 64)
            d1[yy, xl] = dens[core, rows, :] + dr0[rows, :]
    for i in (1, 2, 3):
        yy, dev = y_peer(i)
        send(d1.at[yy], dry.at[y], y_ssem.at[i], y_rsem.at[y], dev)
    first_product(1)

    to_across = []
    for h, rows in enumerate(halves):
        p_across = metric_part(across, rows)
        to_mate[h].wait_recv()
        part[1, rows, :] = p_across + ra[rows, :]
        to_across.append(
            send(
                part.at[1, rows], rx.at[rows], half_ssem.at[1, h], half_rsem.at[1, h], (b, across)
            )
        )

    part[2] = metric_part(mate, everything)
    c_b = send(part.at[2], rb, tail_ssem.at[1], tail_rsem.at[1], (b, mate))

    total = d1[y]
    for i in (1, 2, 3):
        yy, dev = y_peer(i)
        remote(d1.at[yy], dry.at[yy], y_ssem.at[i], y_rsem.at[yy], dev).wait_recv()
        total = total + dry[yy]
    for zz in range(8):
        d2[zz] = total[:, zz * 8 : zz * 8 + 8, :]
    for i in range(1, 8):
        zz, dev = z_peer(i)
        send(d2.at[zz], drz.at[z], z_ssem.at[i], z_rsem.at[z], dev)

    part[3] = metric_part(s, everything)

    total = d2[z]
    for i in range(1, 8):
        zz, dev = z_peer(i)
        remote(d2.at[zz], drz.at[zz], z_ssem.at[i], z_rsem.at[zz], dev).wait_recv()
        total = total + drz[zz]
    d3[...] = total
    here = x_hi * 2 + x_lo
    drx[core, here] = d3[x_lo]
    send(d3.at[x_lo], drx.at[core, here], tail_ssem.at[2], x_rsem.at[core, here], (b, mate))
    for i in (1, 2, 3):
        for c in range(2):
            xx, dev = x_peer(i, c)
            send(
                d3.at[xx % 2], drx.at[core, here], x_ssem.at[c, i], x_rsem.at[core, here], dev
            )

    c_b.wait_recv()
    part[3] = part[3] + rb[...]

    def dens_arrived(c, xx):
        remote(
            d3.at[0], drx.at[c, xx], x_ssem.at[0, 0], x_rsem.at[c, xx], (b, mate)
        ).wait_recv()

    dens_arrived(1 - core, here)
    for i in (1, 2, 3):
        for c in range(2):
            dens_arrived(c, x_peer(i, c)[0])
    for c in range(2):
        row_sum = (drx[c, 0] + drx[c, 1]) + (drx[c, 2] + drx[c, 3])
        for j in range(2):
            out_ref[pl.ds(4 * QW + (2 * c + j) * 8, 8), :] = row_sum[:, j * 128 : j * 128 + 128]

    for h, rows in enumerate(halves):
        to_across[h].wait_recv()
        done = (part[3, rows, :] + rx[rows, :]).T
        for j in range(2):
            out_ref[pl.ds(2 * h + j, QW, stride=4), :] = done[:, j * 128 : j * 128 + 128]

    first_across().wait_send()
    first_mate().wait_send()
    pass_on().wait_send()

    @pl.when(x_hi == 0)
    def _():
        first_up().wait_send()
        first_down().wait_send()
        for way in (1, 0):
            for h in range(2):
                ring_start_r(way, h).wait_send()
            for q in (2, 3):
                ring_start(q, way, jb.at[z, q], q).wait_send()
        for c in to_rows(z, f_ref.at[0]):
            c.wait_send()

    @pl.when(s == 2)
    def _():
        for way in (1, 0):
            for q in range(4):
                ring_start(q, way, jb.at[8, q], q).wait_send()

    @pl.when(s == 3)
    def _():
        chain_up().wait_send()
        chain_down().wait_send()

        @pl.when(z < 7)
        def _():
            chain_start(1).wait_send()

        @pl.when(z > 0)
        def _():
            chain_start(0).wait_send()

    def drain(p, carry):
        slot = slot_of(p)

        @pl.when(x_hi == 0)
        def _():
            for c in to_rows(slot, rbuf.at[slot]):
                c.wait_send()

            @pl.when(goes_on(p, 1 - core))
            def _():
                for h in range(2):
                    ring_hop_r(slot, p % 2, h).wait_send()

            for q, left4 in ((2, 1), (3, 0)):

                @pl.when(goes_on(p, left4))
                def _():
                    ring_hop(slot, q, p % 2).wait_send()

        @pl.when(s == 2)
        def _():
            for q, left4 in ((2, 0), (0, 1), (3, 0), (1, 1)):

                @pl.when(goes_on(p, left4))
                def _():
                    ring_hop(slot, q, p % 2).wait_send()

                if q < 3:
                    to_far_row(slot, q).wait_send()

        @pl.when((s == 3) & (((slot < z) & (z < 7)) | ((slot > z) & (z > 0))))
        def _():
            ring_hop(slot, 3, 0).wait_send()

        return carry

    lax.fori_loop(1, 8, drain, 0)
    for c in sends:
        c.wait_send()


def hand_over(both_ref, gamma_out, dens_out):
    gamma_out[...] = both_ref[: 4 * QW, :]
    for j in range(4):
        dens_out[:, pl.ds(j * 128, 128)] = both_ref[pl.ds(4 * QW + j * 8, 8), :]


def per_device(factors, occ_energy, vir_energy, metric):
    vmem = pl.BlockSpec(memory_space=pltpu.VMEM)
    hbm = pl.BlockSpec(memory_space=pltpu.HBM)
    dma = pltpu.SemaphoreType.DMA
    both = pl.pallas_call(
        kernel,
        out_shape=jax.ShapeDtypeStruct((4 * QW + 32, 128), F32),
        in_specs=[hbm, hbm, hbm, hbm],
        out_specs=vmem,
        scratch_shapes=[
            pltpu.VMEM((9, 4, V, QW), BF16),
            pltpu.VMEM((8, V, QW), BF16),
            pltpu.VMEM((4, V, QW), F32),
            pltpu.VMEM((2, V, QW), F32),
            pltpu.VMEM((V, V), F32),
            pltpu.VMEM((V, V), F32),
            pltpu.VMEM((V, V), BF16),
            pltpu.VMEM((4 * QW, 4 * QW), F32),
            pltpu.VMEM((4 * QW, 4 * QW), BF16),
            pltpu.VMEM((4 * QW, 4 * QW), BF16),
            pltpu.VMEM((4, V, QW), BF16),
            pltpu.VMEM((4, V, QW), BF16),
            pltpu.VMEM((4, V, QW), F32),
            pltpu.VMEM((V, QW), F32),
            pltpu.VMEM((V, QW), F32),
            pltpu.VMEM((V, QW), F32),
            pltpu.VMEM((V, QW), F32),
            pltpu.VMEM((4, 2, 64, QW), F32),
            pltpu.VMEM((4, 2, 64, QW), F32),
            pltpu.VMEM((8, 2, 8, QW), F32),
            pltpu.VMEM((8, 2, 8, QW), F32),
            pltpu.VMEM((2, 8, QW), F32),
            pltpu.VMEM((2, 4, 8, QW), F32),
            pltpu.SMEM((NB,), F32),
            pltpu.VMEM((1, V), F32),
            dma((4,)),
            dma((5,)),
            dma((4, 2)),
            dma((8, 4)),
            dma((8, 2)),
            dma((8, 4)),
            dma((9, 4)),
            dma((8, 2)),
            dma((3,)),
            dma((3,)),
            dma((2, 2)),
            dma((2, 2)),
            dma((4,)),
            dma((4,)),
            dma((8,)),
            dma((8,)),
            dma((2, 4)),
            dma((2, 4)),
        ],
        compiler_params=pltpu.CompilerParams(
            collective_id=0, has_side_effects=True, vmem_limit_bytes=60 * 1024 * 1024
        ),
    )(occ_energy, factors, vir_energy.reshape(1, V), metric)
    gamma, density = pl.pallas_call(
        hand_over,
        out_shape=(
            jax.ShapeDtypeStruct((4 * QW, 128), F32),
            jax.ShapeDtypeStruct((8, V), F32),
        ),
        in_specs=[vmem],
        out_specs=(vmem, vmem),
        compiler_params=pltpu.CompilerParams(vmem_limit_bytes=4 * 1024 * 1024),
    )(both)
    return gamma.reshape(QW, 1, V), density


def solution(mesh):
    return jax.shard_map(
        per_device,
        mesh=mesh,
        in_specs=(P("blk", None, "sec"), P(), P(), P()),
        out_specs=(P("sec", "blk", None), P("blk", None)),
        check_vma=False,
    )
```

```python
import jax
import jax.numpy as jnp
from jax import lax
from jax.experimental import pallas as pl
from jax.experimental.pallas import tpu as pltpu
from jax.sharding import PartitionSpec as P

MESH = pl.DeviceIdType.MESH
F32 = jnp.float32
BF16 = jnp.bfloat16
NT = (((1,), (1,)), ((), ()))
NN = (((1,), (0,)), ((), ()))

V = 512
QW = 256
NB = 64
ROWS = 256


def dot(a, b, dims):
    return lax.dot_general(a, b, dims, preferred_element_type=F32)


def kernel(
    occ_ref,
    f_ref,
    vir_ref,
    metric_ref,
    out_ref,
    jb,
    rbuf,
    g_acc,
    dens,
    vir_sum,
    t_buf,
    tb_buf,
    m_f32,
    m_hi,
    m_lo,
    g_hi,
    g_lo,
    part,
    ra,
    rb,
    rx,
    dr0,
    d1,
    dry,
    d2,
    drz,
    d3,
    drx,
    occ_sm,
    vir_vm,
    local_sem,
    init_ssem,
    zinit_ssem,
    z_fwd,
    zr_fwd,
    y_fwd,
    rsem,
    rrsem,
    tail_ssem,
    tail_rsem,
    half_ssem,
    half_rsem,
    hand_ssem,
    hand_rsem,
    y_ssem,
    y_rsem,
    z_ssem,
    z_rsem,
    x_ssem,
    x_rsem,
):
    b = lax.axis_index("blk")
    s = lax.axis_index("sec")
    x_hi = s // 2
    core = s % 2
    x_lo = b // 32
    y = (b // 8) % 4
    z = b % 8
    mate = s + 1 - 2 * core
    across = (s + 2) % 4
    diag = 3 - s

    def y_peer(i):
        yy = (y + i) % 4
        return yy, (x_lo * 32 + yy * 8 + z, s)

    def z_peer(i):
        zz = (z + i + 8) % 8
        return zz, (x_lo * 32 + y * 8 + zz, s)

    def x_peer(i, to_core):
        xx = (x_hi * 2 + x_lo + i) % 4
        return xx, ((xx % 2) * 32 + y * 8 + z, (xx // 2) * 2 + to_core)

    def row_peer(rows, sec):
        return ((b + 8 * rows + NB) % NB, sec)

    barrier = pltpu.get_barrier_semaphore()

    def greet(dev):
        pl.semaphore_signal(barrier, inc=1, device_id=dev, device_id_type=MESH)

    occ_copy = pltpu.make_async_copy(occ_ref, occ_sm, local_sem.at[2])
    vir_copy = pltpu.make_async_copy(vir_ref, vir_vm, local_sem.at[3])
    metric_copy = pltpu.make_async_copy(metric_ref, m_f32, local_sem.at[1])
    own_copy = pltpu.make_async_copy(f_ref.at[0], jb.at[8, s], local_sem.at[0])

    greet((b, mate))
    for i in (1, 2, 3):
        for c in range(2):
            greet(x_peer(i, c)[1])
    for c in range(2):
        greet(row_peer(1 + x_hi, x_hi * 2 + c))
        greet(row_peer(-1 - x_hi, x_hi * 2 + c))
    for i in (1, 2, 3):
        greet(y_peer(i)[1])
    for i in range(1, 8):
        greet(z_peer(i)[1])

    vir_copy.start()
    occ_copy.start()
    own_copy.start()
    metric_copy.start()
    vir_copy.wait()
    vir_rows = jnp.broadcast_to(vir_vm[...], (V, V))
    vir_sum[...] = vir_rows + vir_rows.T
    g_acc[...] = jnp.zeros_like(g_acc)
    dens[...] = jnp.zeros_like(dens)

    pl.semaphore_wait(barrier, 21)

    def remote(src, dst, send, recv, dev):
        return pltpu.make_async_remote_copy(
            src_ref=src, dst_ref=dst, send_sem=send, recv_sem=recv,
            device_id=dev, device_id_type=MESH,
        )

    def arrived(entry, q):
        remote(
            jb.at[entry, q], jb.at[entry, q], z_fwd.at[0, 0], rsem.at[entry, q], (b, mate)
        ).wait_recv()

    def slot_of(p):
        return (z + ((p + 1) // 2) * (1 - 2 * (p % 2)) + 8) % 8

    def first(i, src, dst, recv, dev):
        return remote(src, dst, init_ssem.at[i], recv, dev)

    def first_across():
        return first(0, f_ref.at[0], jb.at[8, s], rsem.at[8, s], (b, across))

    def first_mate():
        return first(1, f_ref.at[0], jb.at[8, s], rsem.at[8, s], (b, mate))

    def first_up():
        return first(
            2, jb.at[8, across], jb.at[z, across], rsem.at[z, across], row_peer(1, 0)
        )

    def first_down():
        return first(
            3, jb.at[8, across], jb.at[z, across], rsem.at[z, across], row_peer(-1, 1)
        )

    def chain_up():
        return first(2, f_ref.at[0], rbuf.at[1], rrsem.at[1, 0], row_peer(2, 3))

    def chain_down():
        return first(3, f_ref.at[0], rbuf.at[0], rrsem.at[0, 0], row_peer(-2, 3))

    def pass_on():
        return first(4, jb.at[8, across], jb.at[8, across], rsem.at[8, across], (b, mate))

    def ring_start(item, way, src, q):
        return remote(
            src, jb.at[z, q], zinit_ssem.at[item, way], rsem.at[z, q], z_peer(2 * way - 1)[1]
        )

    halves = [pl.ds(h * QW, QW) for h in range(2)]

    def ring_start_r(way, h):
        return remote(
            f_ref.at[0, halves[h]], rbuf.at[z, halves[h]], zinit_ssem.at[h, way],
            rrsem.at[z, h], z_peer(2 * way - 1)[1],
        )

    def chain_start(way):
        return remote(
            rbuf.at[1 - way], jb.at[z, 3], zinit_ssem.at[3, way], rsem.at[z, 3],
            z_peer(2 * way - 1)[1],
        )

    def ring_hop(slot, q, way):
        return remote(
            jb.at[slot, q], jb.at[slot, q], z_fwd.at[slot, q], rsem.at[slot, q],
            z_peer(2 * way - 1)[1],
        )

    def ring_hop_r(slot, way, h):
        return remote(
            rbuf.at[slot, halves[h]], rbuf.at[slot, halves[h]], zr_fwd.at[slot, h],
            rrsem.at[slot, h], z_peer(2 * way - 1)[1],
        )

    def to_rows(slot, src):
        return (
            remote(src, jb.at[slot, s], y_fwd.at[slot, 0], rsem.at[slot, s], row_peer(1, 0)),
            remote(src, jb.at[slot, s], y_fwd.at[slot, 1], rsem.at[slot, s], row_peer(-1, 1)),
        )

    def to_far_row(slot, q):
        up = jnp.where(slot > z, 2, -2)
        return remote(
            jb.at[slot, q], jb.at[slot, q], y_fwd.at[slot, q], rsem.at[slot, q], row_peer(up, 3)
        )

    def goes_on(p, left4):
        d = (p + 1) // 2
        return (d < 3) | ((d == 3) & (p % 2 == left4))

    def relay(p, q, left4):
        slot = slot_of(p)
        arrived(slot, q)

        @pl.when(goes_on(p, left4))
        def _():
            ring_hop(slot, q, p % 2).start()

    def relay_r(p):
        slot = slot_of(p)
        for h in range(2):
            ring_hop_r(slot, 0, h).wait_recv()

            @pl.when(goes_on(p, 1 - core))
            def _():
                ring_hop_r(slot, p % 2, h).start()

    def rows_r(p):
        slot = slot_of(p)
        for c in to_rows(slot, rbuf.at[slot]):
            c.start()

    @pl.when(s == 2)
    def _():
        for way in (1, 0):
            ring_start(2, way, f_ref.at[0], 2).start()

    @pl.when(x_hi == 0)
    def _():
        for h in range(2):
            for way in (1, 0):
                ring_start_r(way, h).start()

    first_across().start()
    first_mate().start()

    @pl.when(x_hi == 0)
    def _():
        for c in to_rows(z, f_ref.at[0]):
            c.start()

    @pl.when(s == 3)
    def _():
        chain_up().start()
        chain_down().start()

    occ_copy.wait()
    own_copy.wait()
    metric_copy.wait()
    for i in range(4):
        rows = pl.ds(i * QW, QW)
        m = m_f32[rows, :]
        hi = m.astype(BF16)
        m_hi[rows, :] = hi
        m_lo[rows, :] = (m - hi.astype(F32)).astype(BF16)

    arrived(8, mate)

    @pl.when(x_hi == 0)
    def _():
        for p in (1, 2):
            relay_r(p)

    @pl.when(s == 2)
    def _():
        for p in (1, 2):
            relay(p, 2, 0)
            to_far_row(slot_of(p), 2).start()

    arrived(8, across)
    pass_on().start()

    @pl.when(x_hi == 0)
    def _():
        first_up().start()
        first_down().start()
        for p in (1, 2):
            rows_r(p)
        for p in (3, 4):
            relay_r(p)
            rows_r(p)

    @pl.when(s == 2)
    def _():
        for way in (1, 0):
            ring_start(0, way, jb.at[8, 0], 0).start()

    arrived(8, diag)

    @pl.when(s == 2)
    def _():
        for q in (1, 3):
            for way in (1, 0):
                ring_start(q, way, jb.at[8, q], q).start()

    @pl.when(s == 3)
    def _():
        for way in (1, 0):
            remote(
                rbuf.at[0], rbuf.at[1 - way], z_fwd.at[0, 0], rrsem.at[1 - way, 0], (b, mate)
            ).wait_recv()

        @pl.when(z < 7)
        def _():
            chain_start(1).start()

        @pl.when(z > 0)
        def _():
            chain_start(0).start()

        def chain(t, carry):
            @pl.when(z - t >= 0)
            def _():
                arrived(z - t, 3)

                @pl.when(z < 7)
                def _():
                    ring_hop(z - t, 3, 1).start()

            @pl.when(z + t < 8)
            def _():
                arrived(z + t, 3)

                @pl.when(z > 0)
                def _():
                    ring_hop(z + t, 3, 0).start()

            return carry

        lax.fori_loop(1, 8, chain, 0)

    own_e = occ_sm[b]

    def pair(entry, other):
        e_sum = own_e + occ_sm[other]
        for rc in range(V // ROWS):
            rows = pl.ds(rc * ROWS, ROWS)
            acc = dot(jb[8, 0, rows, :], jb[entry, 0], NT)
            for q in range(1, 4):
                acc = acc + dot(jb[8, q, rows, :], jb[entry, q], NT)
            t = acc / (e_sum - vir_sum[rows, :])
            t_buf[rows, :] = t
            tb_buf[rows, :] = t.astype(BF16)
        for rc in range(V // ROWS):
            rows = pl.ds(rc * ROWS, ROWS)
            ub = (2.0 * t_buf[rows, :] - t_buf[:, rows].T).astype(BF16)
            for h in range(2):
                dens[h, rows, :] += dot(ub, tb_buf[pl.ds(h * QW, QW), :], NT)
            for q in range(4):
                g_acc[q, rows, :] += dot(ub, jb[entry, q], NN)

    def both_ways(d, q, left4):
        relay(2 * d - 1, q, left4)
        relay(2 * d, q, left4)

    def far_rows(d, q):
        for p in (2 * d - 1, 2 * d):
            to_far_row(slot_of(p), q).start()

    @pl.when(x_hi == 0)
    def _():
        for q in (2, 3):
            arrived(z, q)
            for way in (1, 0):
                ring_start(q, way, jb.at[z, q], q).start()
        for p in (5, 6, 7):
            relay_r(p)
            rows_r(p)

    def handed(i):
        return remote(
            jb.at[slot_of(i + 1)], jb.at[9 + i], hand_ssem.at[i], hand_rsem.at[i], (b, mate)
        )

    def place(p, carry):
        d = (p + 1) // 2
        n = p - 1
        slot = slot_of(n)

        @pl.when((p < 7) & (p % 2 == 1) & (x_hi == 0))
        def _():
            both_ways(d, 2, 1)

        @pl.when((p < 7) & (p % 2 == 0) & (x_hi == 0))
        def _():
            both_ways(d, 3, 0)

        @pl.when((p == 8) & (x_hi == 0))
        def _():
            arrived(slot, 2)
            arrived(slot, 3)

        @pl.when((p < 7) & (p % 2 == 1) & (s == 2))
        def _():
            both_ways(d, 0, 1)
            far_rows(d, 0)

            @pl.when(d < 3)
            def _():
                both_ways(d + 1, 2, 0)
                far_rows(d + 1, 2)

            @pl.when(d == 3)
            def _():
                relay(7, 2, 0)
                to_far_row(slot_of(7), 2).start()

        @pl.when((p < 7) & (p % 2 == 0) & (s == 2))
        def _():
            both_ways(d, 1, 1)
            far_rows(d, 1)
            both_ways(d, 3, 0)

        @pl.when((p == 7) & (s == 2))
        def _():
            for q in (0, 1):
                relay(7, q, 1)
                to_far_row(slot_of(7), q).start()

        @pl.when((p == 8) & (s == 2))
        def _():
            relay(7, 3, 0)

        @pl.when((p < 9) & (x_hi == 0))
        def _():
            arrived(slot, 0)
            arrived(slot, 1)

        @pl.when((n > 3) & (n < 8) & (s == 3))
        def _():
            for q in (2, 0, 1):
                arrived(slot, q)

        @pl.when((n > 7) & (s == 2))
        def _():
            handed(n - 8).wait_recv()

        block = jnp.where(n > 7, slot_of(n - 7), slot)
        shift = jnp.where(s == 0, -1, jnp.where(s == 1, 1, 0))
        shift = jnp.where((s == 3) | (n > 7), jnp.where(block > z, -2, 2), shift)
        other = ((b // 8 + shift + 8) % 8) * 8 + block
        entry = jnp.where((n == 0) & (s == 2), 8, jnp.where(n > 7, n + 1, slot))

        @pl.when(((s != 3) & (n < 8)) | ((s == 3) & (n > 3) & (n < 8)) | ((s == 2) & (n > 7)))
        def _():
            pair(entry, other)

        return carry

    @pl.when(s == 3)
    def _():
        for i in range(3):
            for q in (2, 0, 1):
                arrived(slot_of(i + 1), q)
            handed(i).start()

    lax.fori_loop(1, 12, place, 0)

    @pl.when(s == 3)
    def _():
        for i in range(3):
            handed(i).wait_send()

    sends = []

    def send(src, dst, ss, rs, dev):
        c = remote(src, dst, ss, rs, dev)
        c.start()
        sends.append(c)
        return c

    c_d0 = send(dens.at[1 - core], dr0, tail_ssem.at[0], tail_rsem.at[0], (b, mate))

    for q in range(4):
        g = g_acc[q]
        hi = g.astype(BF16)
        g_hi[q] = hi
        g_lo[q] = (g - hi.astype(F32)).astype(BF16)

    def metric_part(t, rows):
        cols = pl.ds(pl.multiple_of(t * QW, QW), QW)
        acc = None
        for q in range(4):
            depth = pl.ds(q * QW, QW)
            mh = m_hi[depth, cols]
            ml = m_lo[depth, cols]
            gh = g_hi[q, rows, :]
            term = dot(gh, mh, NN) + (dot(g_lo[q, rows, :], mh, NN) + dot(gh, ml, NN))
            acc = term if acc is None else acc + term
        return acc

    everything = pl.ds(0, V)
    to_mate = []

    def first_product(h):
        rows = halves[h]
        part[0, rows, :] = metric_part(diag, rows)
        to_mate.append(
            send(
                part.at[0, rows], ra.at[rows], half_ssem.at[0, h], half_rsem.at[0, h], (b, mate)
            )
        )

    first_product(0)
    c_d0.wait_recv()
    for yy in range(4):
        for xl in range(2):
            rows = pl.ds(xl * 256 + yy * 64, 64)
            d1[yy, xl] = dens[core, rows, :] + dr0[rows, :]
    for i in (1, 2, 3):
        yy, dev = y_peer(i)
        send(d1.at[yy], dry.at[y], y_ssem.at[i], y_rsem.at[y], dev)
    first_product(1)

    to_across = []
    for h, rows in enumerate(halves):
        p_across = metric_part(across, rows)
        to_mate[h].wait_recv()
        part[1, rows, :] = p_across + ra[rows, :]
        to_across.append(
            send(
                part.at[1, rows], rx.at[rows], half_ssem.at[1, h], half_rsem.at[1, h], (b, across)
            )
        )

    part[2] = metric_part(mate, everything)
    c_b = send(part.at[2], rb, tail_ssem.at[1], tail_rsem.at[1], (b, mate))

    total = d1[y]
    for i in (1, 2, 3):
        yy, dev = y_peer(i)
        remote(d1.at[yy], dry.at[yy], y_ssem.at[i], y_rsem.at[yy], dev).wait_recv()
        total = total + dry[yy]
    for zz in range(8):
        d2[zz] = total[:, zz * 8 : zz * 8 + 8, :]
    for i in range(1, 8):
        zz, dev = z_peer(i)
        send(d2.at[zz], drz.at[z], z_ssem.at[i], z_rsem.at[z], dev)

    part[3] = metric_part(s, everything)

    total = d2[z]
    for i in range(1, 8):
        zz, dev = z_peer(i)
        remote(d2.at[zz], drz.at[zz], z_ssem.at[i], z_rsem.at[zz], dev).wait_recv()
        total = total + drz[zz]
    d3[...] = total
    here = x_hi * 2 + x_lo
    drx[core, here] = d3[x_lo]
    send(d3.at[x_lo], drx.at[core, here], tail_ssem.at[2], x_rsem.at[core, here], (b, mate))
    for i in (1, 2, 3):
        for c in range(2):
            xx, dev = x_peer(i, c)
            send(
                d3.at[xx % 2], drx.at[core, here], x_ssem.at[c, i], x_rsem.at[core, here], dev
            )

    c_b.wait_recv()
    part[3] = part[3] + rb[...]

    def dens_arrived(c, xx):
        remote(
            d3.at[0], drx.at[c, xx], x_ssem.at[0, 0], x_rsem.at[c, xx], (b, mate)
        ).wait_recv()

    dens_arrived(1 - core, here)
    for i in (1, 2, 3):
        for c in range(2):
            dens_arrived(c, x_peer(i, c)[0])
    for c in range(2):
        row_sum = (drx[c, 0] + drx[c, 1]) + (drx[c, 2] + drx[c, 3])
        for j in range(2):
            out_ref[pl.ds(4 * QW + (2 * c + j) * 8, 8), :] = row_sum[:, j * 128 : j * 128 + 128]

    for h, rows in enumerate(halves):
        to_across[h].wait_recv()
        done = (part[3, rows, :] + rx[rows, :]).T
        for j in range(2):
            out_ref[pl.ds(2 * h + j, QW, stride=4), :] = done[:, j * 128 : j * 128 + 128]

    first_across().wait_send()
    first_mate().wait_send()
    pass_on().wait_send()

    @pl.when(x_hi == 0)
    def _():
        first_up().wait_send()
        first_down().wait_send()
        for way in (1, 0):
            for h in range(2):
                ring_start_r(way, h).wait_send()
            for q in (2, 3):
                ring_start(q, way, jb.at[z, q], q).wait_send()
        for c in to_rows(z, f_ref.at[0]):
            c.wait_send()

    @pl.when(s == 2)
    def _():
        for way in (1, 0):
            for q in range(4):
                ring_start(q, way, jb.at[8, q], q).wait_send()

    @pl.when(s == 3)
    def _():
        chain_up().wait_send()
        chain_down().wait_send()

        @pl.when(z < 7)
        def _():
            chain_start(1).wait_send()

        @pl.when(z > 0)
        def _():
            chain_start(0).wait_send()

    def drain(p, carry):
        slot = slot_of(p)

        @pl.when(x_hi == 0)
        def _():
            for c in to_rows(slot, rbuf.at[slot]):
                c.wait_send()

            @pl.when(goes_on(p, 1 - core))
            def _():
                for h in range(2):
                    ring_hop_r(slot, p % 2, h).wait_send()

            for q, left4 in ((2, 1), (3, 0)):

                @pl.when(goes_on(p, left4))
                def _():
                    ring_hop(slot, q, p % 2).wait_send()

        @pl.when(s == 2)
        def _():
            for q, left4 in ((2, 0), (0, 1), (3, 0), (1, 1)):

                @pl.when(goes_on(p, left4))
                def _():
                    ring_hop(slot, q, p % 2).wait_send()

                if q < 3:
                    to_far_row(slot, q).wait_send()

        @pl.when((s == 3) & (((slot < z) & (z < 7)) | ((slot > z) & (z > 0))))
        def _():
            ring_hop(slot, 3, 0).wait_send()

        return carry

    lax.fori_loop(1, 8, drain, 0)
    for c in sends:
        c.wait_send()


def hand_over(both_ref, gamma_out, dens_out):
    gamma_out[...] = both_ref[: 4 * QW, :]
    for j in range(4):
        dens_out[:, pl.ds(j * 128, 128)] = both_ref[pl.ds(4 * QW + j * 8, 8), :]


def per_device(factors, occ_energy, vir_energy, metric):
    vmem = pl.BlockSpec(memory_space=pltpu.VMEM)
    hbm = pl.BlockSpec(memory_space=pltpu.HBM)
    dma = pltpu.SemaphoreType.DMA
    both = pl.pallas_call(
        kernel,
        out_shape=jax.ShapeDtypeStruct((4 * QW + 32, 128), F32),
        in_specs=[hbm, hbm, hbm, hbm],
        out_specs=vmem,
        scratch_shapes=[
            pltpu.VMEM((12, 4, V, QW), BF16),
            pltpu.VMEM((8, V, QW), BF16),
            pltpu.VMEM((4, V, QW), F32),
            pltpu.VMEM((2, V, QW), F32),
            pltpu.VMEM((V, V), F32),
            pltpu.VMEM((V, V), F32),
            pltpu.VMEM((V, V), BF16),
            pltpu.VMEM((4 * QW, 4 * QW), F32),
            pltpu.VMEM((4 * QW, 4 * QW), BF16),
            pltpu.VMEM((4 * QW, 4 * QW), BF16),
            pltpu.VMEM((4, V, QW), BF16),
            pltpu.VMEM((4, V, QW), BF16),
            pltpu.VMEM((4, V, QW), F32),
            pltpu.VMEM((V, QW), F32),
            pltpu.VMEM((V, QW), F32),
            pltpu.VMEM((V, QW), F32),
            pltpu.VMEM((V, QW), F32),
            pltpu.VMEM((4, 2, 64, QW), F32),
            pltpu.VMEM((4, 2, 64, QW), F32),
            pltpu.VMEM((8, 2, 8, QW), F32),
            pltpu.VMEM((8, 2, 8, QW), F32),
            pltpu.VMEM((2, 8, QW), F32),
            pltpu.VMEM((2, 4, 8, QW), F32),
            pltpu.SMEM((NB,), F32),
            pltpu.VMEM((1, V), F32),
            dma((4,)),
            dma((5,)),
            dma((4, 2)),
            dma((8, 4)),
            dma((8, 2)),
            dma((8, 4)),
            dma((9, 4)),
            dma((8, 2)),
            dma((3,)),
            dma((3,)),
            dma((2, 2)),
            dma((2, 2)),
            dma((3,)),
            dma((3,)),
            dma((4,)),
            dma((4,)),
            dma((8,)),
            dma((8,)),
            dma((2, 4)),
            dma((2, 4)),
        ],
        compiler_params=pltpu.CompilerParams(
            collective_id=0, has_side_effects=True, vmem_limit_bytes=60 * 1024 * 1024
        ),
    )(occ_energy, factors, vir_energy.reshape(1, V), metric)
    gamma, density = pl.pallas_call(
        hand_over,
        out_shape=(
            jax.ShapeDtypeStruct((4 * QW, 128), F32),
            jax.ShapeDtypeStruct((8, V), F32),
        ),
        in_specs=[vmem],
        out_specs=(vmem, vmem),
        compiler_params=pltpu.CompilerParams(vmem_limit_bytes=4 * 1024 * 1024),
    )(both)
    return gamma.reshape(QW, 1, V), density


def solution(mesh):
    return jax.shard_map(
        per_device,
        mesh=mesh,
        in_specs=(P("blk", None, "sec"), P(), P(), P()),
        out_specs=(P("sec", "blk", None), P("blk", None)),
        check_vma=False,
    )
```
